32 devices in a mesh: member: 2 (over x), gx: 16 (over z, y, core).
Axes of the slice: x: 2, y: 2, z: 4, core: 2. Of those that a mesh axis runs over, the one named last changes fastest.
Arguments:
- electric: float32 [3, 64, 256, 128], P(None, 'gx'), may hold values from -6 to 6
- magnetic: float32 [3, 64, 256, 128], P(None, 'gx'), may hold values from -6 to 6
- material: int32 [128, 256, 128], P(('member', 'gx')), parts along dimension 0, may hold values from 0 to 3, as said below
- permittivity: float32 [4], replicated, may hold values from 1 to 4
- pole_frequency: float32 [2], replicated, may hold values from 0.3 to 1.2
- pole_damping: float32 [2], replicated, may hold values from 0.05 to 1
- pole_strength: float32 [2], replicated, may hold values from 0.3 to 2
- frequencies: float32 [8], replicated, may hold values from 0.2 to 2
- plane_depth: int32 [4], replicated, may hold values from 1 to 126
- mode_fields: float32 [4, 4, 64, 256], P(None, None, 'gx'), may hold values from -40 to 40
Outputs:
- electric_final: float32 [3, 128, 256, 128], P(None, ('member', 'gx')), parts along dimension 1
- magnetic_final: float32 [3, 128, 256, 128], P(None, ('member', 'gx')), parts along dimension 1
- monitors: float32 [2, 4, 8, 4, 128, 256], P(None, None, None, None, ('member', 'gx')), parts along dimension 4
- intersection: float32 [4, 4, 8], P('member'), parts along dimension 0
The draws below stay inside these ranges and needn't reach their ends.
There are 2 independent parts, one for each index of `member`. The reference program is written for one: setup_inputs(seed, part) draws one part's arguments, and reference() takes and returns one part's arrays. A program takes and returns all parts, laid end to end along the dimension named above; an argument that names none is the same for every part. Nothing has to cross between parts.
Inputs may be any that keep to these rules, and one draw needn't show every extreme that they name: Each 16-layer thickness profile stacks layers along the first dimension, each of one material, with a lateral lattice of material 0 cells in some layers; materials 2 and above are dispersive.
All inputs are finite; a program needn't handle non-finite values.
Results may differ from the reference program's by a relative error of at most 0.0003.
Values sent between devices are 32-bit elements; how exact they have to be, the bound alone decides.
A program may use at most 64 MiB of HBM per device.

```python
import math
import jax
import jax.numpy as jnp
from jax import lax

NY = 256
NZ = 128
STEPS = 6
NF = 8
NMON = 4
LAYERS = 16
NMAT = 4
NPOLE = 2
NX = 64


def draw_material(key, part):
    keys = jax.random.split(jax.random.fold_in(key, 11), 4)
    cuts = jax.random.permutation(keys[0], NX - 1)[:LAYERS - 1] + 1
    position = jnp.arange(NX, dtype=jnp.int32)
    layer = jnp.sum((position[:, None] >= cuts[None, :]).astype(jnp.int32), axis=1)
    layer_kind = (jax.random.permutation(keys[1], LAYERS) % NMAT).astype(jnp.int32)
    patterned = jax.random.randint(keys[2], (LAYERS,), 0, 2)
    holes = jax.random.randint(keys[3], (NY, NZ), 0, 2)
    kind_cells = jnp.take(layer_kind, layer)
    drilled = jnp.take(patterned, layer)
    filled = kind_cells[:, None, None] * jnp.ones((1, NY, NZ), jnp.int32)
    return jnp.where(drilled[:, None, None] * holes[None, :, :] > 0, 0, filled).astype(jnp.int32)


def draw_mode_fields(key, part):
    ramp = 1.0 + 2.0 * jnp.arange(NX, dtype=jnp.float32) / (NX - 1.0)
    base = jnp.clip(jax.random.normal(jax.random.fold_in(key, 7), (4, NMON, NX, NY), jnp.float32), -4.0, 4.0)
    return base * ramp[None, None, :, None]


def set_ends(result, own_key, low, largest):
    longest = result.shape.index(max(result.shape))
    spots = []
    for shift in (0, 1):
        where = [jax.random.randint(jax.random.fold_in(own_key, axis), (), 0, length) for axis, length in enumerate(result.shape)]
        where[longest] = (where[longest] + shift) % result.shape[longest]
        spots.append(tuple(where))
    return result.at[spots[0]].set(low).at[spots[1]].set(largest)


def shard_levels(own_key, shape, cuts, low, top_value):
    gain, own = 1.0, jax.random.fold_in(own_key, 6)
    for dim, parts in cuts:
        steps = jnp.exp(jax.random.uniform(jax.random.fold_in(own, dim), (parts,), jnp.float32, low / len(cuts), top_value / len(cuts)))
        gain = gain * jnp.repeat(steps, shape[dim] // parts).reshape([-1 if axis == dim else 1 for axis in range(len(shape))])
    return gain


def noise(rng, extent, scale, reach, shards=(), kind=jnp.bfloat16):
    entries = scale * jax.random.normal(rng, extent, jnp.float32)
    if shards:
        entries = entries * shard_levels(rng, extent, shards, -0.22, 0.18)
    return jnp.clip(entries, -reach, reach).astype(kind)


def setup_inputs(seed: int = 0, part: int = 0) -> dict:
    arg_keys = jax.random.split(jax.random.key(seed), 11)
    part_keys = jax.random.split(jax.random.fold_in(arg_keys[10], part), 11)
    return {
        "electric": noise(arg_keys[0], (3, NX, NY, NZ), 1.0, 6.0, ((1, 16),), jnp.float32),
        "magnetic": noise(arg_keys[1], (3, NX, NY, NZ), 1.0, 6.0, ((1, 16),), jnp.float32),
        "material": draw_material(jax.random.fold_in(jax.random.fold_in(arg_keys[10], part), 71), part),
        "permittivity": jnp.clip(jax.random.uniform(arg_keys[3], (NMAT,), jnp.float32, 1.0, 4.0), 1.0, 4.0),
        "pole_frequency": jnp.clip(jnp.exp(jax.random.uniform(arg_keys[4], (NPOLE,), jnp.float32, math.log(0.3), math.log(1.2))), 0.3, 1.2),
        "pole_damping": jnp.clip(jnp.exp(jax.random.uniform(arg_keys[5], (NPOLE,), jnp.float32, math.log(0.05), math.log(1.0))), 0.05, 1.0),
        "pole_strength": jnp.clip(jnp.exp(jax.random.uniform(arg_keys[6], (NPOLE,), jnp.float32, math.log(0.3), math.log(2.0))), 0.3, 2.0),
        "frequencies": jnp.clip(jnp.exp(jax.random.uniform(arg_keys[7], (NF,), jnp.float32, math.log(0.2), math.log(2.0))), 0.2, 2.0),
        "plane_depth": set_ends(jax.random.randint(arg_keys[8], (NMON,), 1, NZ - 1), jax.random.fold_in(arg_keys[8], 1), 1, (NZ - 1) - 1).astype(jnp.int32),
        "mode_fields": draw_mode_fields(jax.random.fold_in(arg_keys[10], 71), part),
    }


DT = 0.5

def zero_rim(field, direction):
    return jnp.zeros_like(lax.slice_in_dim(field, 0, 1, axis=direction))

def diff_ahead(field, direction, beyond):
    remainder = lax.slice_in_dim(field, 1, field.shape[direction], axis=direction)
    return jnp.concatenate([remainder, beyond], axis=direction) - field

def diff_behind(field, direction, preceding):
    remainder = lax.slice_in_dim(field, 0, field.shape[direction] - 1, axis=direction)
    return field - jnp.concatenate([preceding, remainder], axis=direction)

def ahead_open(field, direction):
    return diff_ahead(field, direction, zero_rim(field, direction))

def behind_open(field, direction):
    return diff_behind(field, direction, zero_rim(field, direction))

def curl_e(e_field, upper):
    first = ahead_open(e_field[2], 1) - ahead_open(e_field[1], 2)
    second = ahead_open(e_field[0], 2) - diff_ahead(e_field[2], 0, upper[1])
    third = diff_ahead(e_field[1], 0, upper[0]) - ahead_open(e_field[0], 1)
    return jnp.stack([first, second, third])

def curl_h(h_field, lower):
    first = behind_open(h_field[2], 1) - behind_open(h_field[1], 2)
    second = behind_open(h_field[0], 2) - diff_behind(h_field[2], 0, lower[1])
    third = diff_behind(h_field[1], 0, lower[0]) - behind_open(h_field[0], 1)
    return jnp.stack([first, second, third])

def coefficients(material, permittivity, pole_frequency, pole_damping, pole_strength):
    eps_cell = jnp.zeros(material.shape, jnp.float32)
    for kind_index in range(permittivity.shape[0]):
        eps_cell = eps_cell + jnp.where(material == kind_index, permittivity[kind_index], 0.0)
    damping = jnp.zeros(material.shape, jnp.float32)
    square = jnp.zeros(material.shape, jnp.float32)
    driving = jnp.zeros(material.shape, jnp.float32)
    offset = permittivity.shape[0] - pole_frequency.shape[0]
    for pole_index in range(pole_frequency.shape[0]):
        chosen = material == pole_index + offset
        freq_sq = pole_frequency[pole_index] * pole_frequency[pole_index]
        damping = damping + jnp.where(chosen, pole_damping[pole_index], 0.0)
        square = square + jnp.where(chosen, freq_sq, 0.0)
        driving = driving + jnp.where(chosen, pole_strength[pole_index] * freq_sq, 0.0)
    divisor = 1.0 + 0.5 * DT * damping
    retain = (1.0 - 0.5 * DT * damping) / divisor
    pulling = DT * driving / divisor
    spring = DT * square / divisor
    step_e = DT / eps_cell
    return (retain, pulling, spring, step_e)

def record(monitors, e_field, h_field, select, frequencies, step):
    plane_e = jnp.einsum('cxyz,zm->cmxy', e_field[:2], select, precision=lax.Precision.HIGHEST)
    plane_h = jnp.einsum('cxyz,zm->cmxy', h_field[:2], select, precision=lax.Precision.HIGHEST)
    planes = jnp.concatenate([plane_e, plane_h], axis=0)
    phase_e = (step + 1.0) * DT * frequencies
    phase_h = (step + 0.5) * DT * frequencies
    cosines = jnp.stack([jnp.cos(phase_e), jnp.cos(phase_e), jnp.cos(phase_h), jnp.cos(phase_h)])
    sine_part = -jnp.stack([jnp.sin(phase_e), jnp.sin(phase_e), jnp.sin(phase_h), jnp.sin(phase_h)])
    rotation = jnp.stack([cosines, sine_part])
    return monitors + rotation[:, :, :, None, None, None] * planes[None, :, None, :, :, :]

def project(monitors, mode_fields, scale):
    pairing = jnp.stack([mode_fields[3], -mode_fields[2], -mode_fields[1], mode_fields[0]])
    return scale * jnp.einsum('rcfmxy,cmxy->rmf', monitors, pairing, precision=lax.Precision.HIGHEST)

def reference(electric, magnetic, material, permittivity, pole_frequency, pole_damping, pole_strength, frequencies, plane_depth, mode_fields):
    retain, pulling, spring, step_e = coefficients(material, permittivity, pole_frequency, pole_damping, pole_strength)
    select = (jnp.arange(NZ)[:, None] == plane_depth[None, :]).astype(jnp.float32)
    boundary = jnp.zeros((2, 1, NY, NZ), jnp.float32)
    current = jnp.zeros_like(electric)
    polarized = jnp.zeros_like(electric)
    monitors = jnp.zeros((2, 4, NF, NMON, NX, NY), jnp.float32)
    for step in range(STEPS):
        magnetic = magnetic - DT * curl_e(electric, boundary)
        current = retain * current + pulling * electric - spring * polarized
        polarized = polarized + DT * current
        electric = electric + step_e * (curl_h(magnetic, boundary) - current)
        monitors = record(monitors, electric, magnetic, select, frequencies, step)
    intersection = project(monitors, mode_fields, 1.0 / math.sqrt(4.0 * NX * NY))
    return (electric, magnetic, monitors, intersection)
```

```python
import functools
import math

import jax
import jax.numpy as jnp
from jax import lax
from jax.experimental import pallas as pl
from jax.experimental.pallas import tpu as pltpu
from jax.sharding import PartitionSpec as P

STEPS = 6
DT = 0.5
CHUNKS = 8
ROWS = 32
PAD = 8
MESH = pl.DeviceIdType.MESH
VMEM_BYTES = 67043328
F32 = jnp.float32
BF16 = jnp.bfloat16


def ahead(value):
    width = value.shape[-1]
    lane = lax.broadcasted_iota(jnp.int32, value.shape, 1)
    return jnp.where(lane == width - 1, 0.0, pltpu.roll(value, width - 1, 1))


def behind(value):
    lane = lax.broadcasted_iota(jnp.int32, value.shape, 1)
    return jnp.where(lane == 0, 0.0, pltpu.roll(value, 1, 1))


def main_kernel(
    count,
    scale,
    perm_ref,
    freq_ref,
    damp_ref,
    strength_ref,
    omega_ref,
    depth_ref,
    mode_ref,
    el_ref,
    ma_ref,
    mat_ref,
    eb,
    hb,
    mon_ref,
    inter_ref,
    ge,
    gh,
    ph,
    jb,
    pb,
    coef,
    matb,
    planes,
    pick,
    part,
    gathered,
    rot,
    rot_s,
    in_sem,
    rot_sem,
    se_sem,
    re_sem,
    sh_sem,
    rh_sem,
    sp_sem,
    rp_sem,
    met_sem,
):
    me = lax.axis_index("gx")
    layers, width, deep = mat_ref.shape
    nm, nf = depth_ref.shape[0], omega_ref.shape[0]
    chunk = width // CHUNKS
    has_upper = me < count - 1
    has_lower = me > 0
    top = layers - 1

    barrier = pltpu.get_barrier_semaphore()
    for present, side in ((has_lower, me - 1), (has_upper, me + 1)):

        @pl.when(present)
        def _(side=side):
            pl.semaphore_signal(barrier, inc=1, device_id={"gx": side}, device_id_type=MESH)

    rest = pl.ds(0, top)
    loads = [
        pltpu.make_async_copy(el_ref.at[:, top], eb.at[:, top, pl.ds(0, width)], in_sem.at[0]),
        pltpu.make_async_copy(ma_ref.at[:, top], hb.at[:, top, pl.ds(PAD, width)], in_sem.at[1]),
        pltpu.make_async_copy(mat_ref, matb, in_sem.at[2]),
        pltpu.make_async_copy(
            el_ref.at[:, rest], eb.at[:, rest, pl.ds(0, width)], in_sem.at[3]
        ),
        pltpu.make_async_copy(
            ma_ref.at[:, rest], hb.at[:, rest, pl.ds(PAD, width)], in_sem.at[4]
        ),
    ]
    for load in loads:
        load.start()

    def send_e(c, source, slot):
        rows = pl.ds(c * chunk, chunk)
        return pltpu.make_async_remote_copy(
            src_ref=source.at[pl.ds(1, 2), 0, rows],
            dst_ref=ge.at[slot, :, rows],
            send_sem=se_sem.at[c],
            recv_sem=re_sem.at[slot, c],
            device_id={"gx": me - 1},
            device_id_type=MESH,
        )

    def send_h(c, slot):
        rows = pl.ds(c * chunk, chunk)
        return pltpu.make_async_remote_copy(
            src_ref=ph.at[:, rows],
            dst_ref=gh.at[slot, :, rows],
            send_sem=sh_sem.at[c],
            recv_sem=rh_sem.at[slot, c],
            device_id={"gx": me + 1},
            device_id_type=MESH,
        )

    zero_rows = jnp.zeros((PAD, deep), F32)
    for c in range(3):
        for x in range(layers):
            eb[c, x, pl.ds(width, PAD), :] = zero_rows
            hb[c, x, pl.ds(0, PAD), :] = zero_rows
    part[...] = jnp.zeros_like(part)

    pl.semaphore_wait(barrier, has_lower.astype(jnp.int32) + has_upper.astype(jnp.int32))

    @pl.when(has_lower)
    def _():
        for c in range(CHUNKS):
            send_e(c, el_ref, 0).start()

    @pl.when(~has_upper)
    def _():
        ge[...] = jnp.zeros_like(ge)

    @pl.when(~has_lower)
    def _():
        gh[...] = jnp.zeros_like(gh)

    def partial_h(y, size):
        here, next_y, spot = pl.ds(y, size), pl.ds(y + 1, size), pl.ds(y + PAD, size)
        ex, ey, ez = eb[0, top, here, :], eb[1, top, here, :], eb[2, top, here, :]
        ex_y = eb[0, top, next_y, :]
        ph[0, here, :] = hb[1, top, spot, :] - DT * ((ahead(ex) - ex) + ez)
        ph[1, here, :] = hb[2, top, spot, :] + DT * (ey + (ex_y - ex))

    loads[0].wait()
    loads[1].wait()
    for c in range(CHUNKS):
        partial_h(c * chunk, chunk)

        @pl.when(has_upper)
        def _(c=c):
            send_h(c, 0).start()

    shape = pick.shape
    row = lax.broadcasted_iota(jnp.int32, shape, 0)
    col = lax.broadcasted_iota(jnp.int32, shape, 1)
    wanted = jnp.zeros(shape, jnp.int32)
    for m in range(nm):
        wanted = jnp.where(row // 8 == m, depth_ref[m], wanted)
    hit = (row % 8 == col // (2 * deep)) & (col % deep == wanted)
    pick[...] = jnp.where(hit, 1.0, 0.0).astype(BF16)

    lane = lax.broadcasted_iota(jnp.int32, (nf, deep), 1)
    line = lax.broadcasted_iota(jnp.int32, (nf, deep), 0)
    omega = jnp.zeros((nf, deep), F32)
    for f in range(nf):
        omega = jnp.where(line == f, omega_ref[f], omega)
    late = jnp.where(lane % 4 < 2, 1.0, 0.5)
    phase = ((lane // 4).astype(F32) + late) * DT * omega
    rot[0] = jnp.where(lane < 4 * STEPS, jnp.cos(phase), 0.0)
    rot[1] = jnp.where(lane < 4 * STEPS, -jnp.sin(phase), 0.0)

    kinds = perm_ref.shape[0]
    offset = kinds - freq_ref.shape[0]
    ones = jnp.ones((8, deep), F32)
    tables = []
    for kind in range(kinds):
        if kind < offset:
            g, w2, drive = 0.0 * ones, 0.0 * ones, 0.0 * ones
        else:
            p = kind - offset
            g = damp_ref[p] * ones
            w2 = (freq_ref[p] * ones) * freq_ref[p]
            drive = strength_ref[p] * w2
        divisor = 1.0 + 0.5 * DT * g
        tables.append(
            (
                (1.0 - 0.5 * DT * g) / divisor,
                DT * drive / divisor,
                DT * w2 / divisor,
                DT / (perm_ref[kind] * ones),
            )
        )

    loads[2].wait()
    for x in range(layers):

        def fill(b, carry, x=x):
            rows = pl.ds(pl.multiple_of(b * 8, 8), 8)
            q = matb[x, rows, :]
            for i in range(4):
                value = tables[0][i]
                for kind in range(1, kinds):
                    value = jnp.where(q == kind, tables[kind][i], value)
                coef[i, x, rows, :] = value
            zero = jnp.zeros_like(ones)
            for c in range(3):
                jb[c, x, rows, :] = zero
                pb[c, x, rows, :] = zero
            return carry

        lax.fori_loop(0, width // 8, fill, 0, unroll=2)

    loads[3].wait()
    loads[4].wait()

    lower = jnp.where(has_lower, DT, 0.0)

    def update_h(x, y, size):
        here, next_y = pl.ds(y, size), pl.ds(y + 1, size)
        spot = pl.ds(y + PAD, size)
        ex, ey, ez = eb[0, x, here, :], eb[1, x, here, :], eb[2, x, here, :]
        ex_y, ez_y = eb[0, x, next_y, :], eb[2, x, next_y, :]
        hb[0, x, spot, :] -= DT * ((ez_y - ez) - (ahead(ey) - ey))
        if x < top:
            ey_x, ez_x = eb[1, x + 1, here, :], eb[2, x + 1, here, :]
            hb[1, x, spot, :] -= DT * ((ahead(ex) - ex) - (ez_x - ez))
            hb[2, x, spot, :] -= DT * ((ey_x - ey) - (ex_y - ex))

    def finish_h(slot, y, size):
        here, spot = pl.ds(y, size), pl.ds(y + PAD, size)
        hb[1, top, spot, :] = ph[0, here, :] + DT * ge[slot, 1, here, :]
        hb[2, top, spot, :] = ph[1, here, :] - DT * ge[slot, 0, here, :]

    def update_e(x, y, size, slot):
        here = pl.ds(y, size)
        spot, last_y = pl.ds(y + PAD, size), pl.ds(y + PAD - 1, size)
        hx, hy, hz = hb[0, x, spot, :], hb[1, x, spot, :], hb[2, x, spot, :]
        hx_y, hz_y = hb[0, x, last_y, :], hb[2, x, last_y, :]
        if x > 0:
            dz = hz - hb[2, x - 1, spot, :]
            dy = hy - hb[1, x - 1, spot, :]
        else:
            dz = hz - (gh[slot, 1, here, :] - lower * eb[1, 0, here, :])
            dy = hy - (gh[slot, 0, here, :] + lower * eb[2, 0, here, :])
        curl = (
            (hz - hz_y) - (hy - behind(hy)),
            (hx - behind(hx)) - dz,
            dy - (hx - hx_y),
        )
        retain, pulling = coef[0, x, here, :], coef[1, x, here, :]
        spring, step_e = coef[2, x, here, :], coef[3, x, here, :]
        for c in range(3):
            field, polar = eb[c, x, here, :], pb[c, x, here, :]
            current = retain * jb[c, x, here, :] + pulling * field - spring * polar
            jb[c, x, here, :] = current
            pb[c, x, here, :] = polar + DT * current
            eb[c, x, here, :] = field + step_e * (curl[c] - current)

    def sweep(update, xs, c, *args):
        size = min(ROWS, chunk)
        for x in xs:
            for y in range(c * chunk, (c + 1) * chunk, size):
                update(x, y, size, *args)

    def record(n, part_of, buf, base, source, c):
        size = width // 2
        cols = pl.ds(part_of * size, size)
        total = jnp.zeros((pick.shape[0], size), F32)
        for x in range(layers):
            value = buf[source, x, pl.ds(base + part_of * size, size), :]
            high = value.astype(BF16)
            low = (value - high.astype(F32)).astype(BF16)
            total = total + lax.dot_general(
                pick[:, pl.ds(x * 2 * deep, 2 * deep)],
                jnp.concatenate([high, low], axis=1),
                (((1,), (1,)), ((), ())),
                preferred_element_type=F32,
            )
        planes[n, c, :, cols] = total
        sums = []
        for m in range(nm):
            product = total[8 * m : 8 * m + layers, :] * mode_ref[3 - c, m, :, cols]
            sums.append(jnp.sum(product, axis=0, keepdims=True))
        value = jnp.sum(jnp.concatenate(sums, axis=0), axis=1, keepdims=True)
        value = value if c in (0, 3) else -value
        here = lax.broadcasted_iota(jnp.int32, (nm, deep), 1) == n * 4 + c
        kept = part[pl.ds(0, nm), :]
        part[pl.ds(0, nm), :] = kept + jnp.where(here, value, 0.0)

    def record_all(n, part_of):
        for c in range(2):
            record(n, part_of, eb, 0, c, c)
            record(n, part_of, hb, PAD, c, 2 + c)

    reach = [d for d in (4 << i for i in range(count.bit_length())) if d < count]

    def greet(i):
        for present, side in ((me >= reach[i], me - reach[i]), (me < count - reach[i], me + reach[i])):

            @pl.when(present)
            def _(side=side):
                pl.semaphore_signal(
                    met_sem.at[i], inc=1, device_id={"gx": side}, device_id_type=MESH
                )

    def met(i):
        peers = sum(p.astype(jnp.int32) for p in (me >= reach[i], me < count - reach[i]))
        pl.semaphore_wait(met_sem.at[i], peers)

    def send_up(n, c, slot):
        @pl.when(has_upper)
        def _():
            send_h(c, slot).wait_send()

        @pl.when(n < STEPS - 1)
        def _():
            partial_h(c * chunk, chunk)

            @pl.when(has_upper)
            def _():
                send_h(c, slot).start()

    def step(n, carry):
        slot = lax.rem(n, 2)
        other = 1 - slot
        for c in range(CHUNKS):
            sweep(update_h, range(layers), c)

            @pl.when(has_upper)
            def _(c=c):
                send_e(c, eb, slot).wait_recv()

            @pl.when(has_lower)
            def _(c=c):
                send_h(c, slot).wait_recv()
                send_e(c, eb, slot).wait_send()

            finish_h(slot, c * chunk, chunk)
            sweep(update_e, (0, top), c, slot)

            @pl.when(has_lower & (n < STEPS - 1))
            def _(c=c):
                send_e(c, eb, other).start()

            if c > 0:
                send_up(n, c - 1, other)
            sweep(update_e, range(1, top), c, slot)
            if c == CHUNKS // 2 - 1:
                record_all(n, 0)
        send_up(n, CHUNKS - 1, other)
        record_all(n, 1)
        for i in range(min(len(reach), STEPS - 3)):

            @pl.when(n == i + 2)
            def _(i=i):
                if i > 0:
                    met(i - 1)
                greet(i)

        return carry

    lax.fori_loop(0, STEPS, step, 0)

    begun = min(len(reach), STEPS - 3)
    for i in range(max(begun - 1, 0), len(reach)):
        if i >= begun:
            greet(i)
        met(i)

    def share(k, slot):
        return pltpu.make_async_remote_copy(
            src_ref=part,
            dst_ref=gathered.at[slot],
            send_sem=sp_sem.at[k],
            recv_sem=rp_sem.at[k],
            device_id={"gx": lax.rem(me + k, count)},
            device_id_type=MESH,
        )

    for k in range(1, count):
        share(k, me).start()
    gathered[me] = part[...]

    to_scalars = pltpu.make_async_copy(rot, rot_s, rot_sem)
    to_scalars.start()

    to_scalars.wait()
    for c in range(4):

        def fold(m, carry, c=c):
            rows = pl.ds(pl.multiple_of(8 * m, 8), layers)
            plane = [planes[n, c, rows, :] for n in range(STEPS)]
            for r in range(2):
                for f in range(nf):
                    value = rot_s[r, f, c] * plane[0]
                    for n in range(1, STEPS):
                        value = value + rot_s[r, f, n * 4 + c] * plane[n]
                    mon_ref[r, c, f, m] = value
            return carry

        lax.fori_loop(0, nm, fold, 0)

    for k in range(1, count):
        share(k, lax.rem(me - k + count, count)).wait()
    full = gathered[0]
    for k in range(1, count):
        full = full + gathered[k]
    for r in range(2):
        out = lax.dot_general(
            full,
            rot[r],
            (((1,), (1,)), ((), ())),
            preferred_element_type=F32,
            precision=lax.Precision.HIGHEST,
        )
        inter_ref[r] = scale * out[:nm, :]


def place_kernel(eb, hb, mon, inter, el_out, ma_out, mon_out, inter_out, sems):
    width = el_out.shape[2]
    copies = [
        pltpu.make_async_copy(eb.at[:, :, pl.ds(0, width)], el_out, sems.at[0]),
        pltpu.make_async_copy(hb.at[:, :, pl.ds(PAD, width)], ma_out, sems.at[1]),
        pltpu.make_async_copy(mon, mon_out, sems.at[2]),
        pltpu.make_async_copy(inter, inter_out, sems.at[3]),
    ]
    for copy in copies:
        copy.start()
    for copy in copies:
        copy.wait()


def on_device(
    electric,
    magnetic,
    material,
    permittivity,
    pole_frequency,
    pole_damping,
    pole_strength,
    frequencies,
    plane_depth,
    mode_fields,
):
    count = lax.axis_size("gx")
    layers, width, deep = material.shape
    nm, nf = plane_depth.shape[0], frequencies.shape[0]
    scale = 1.0 / math.sqrt(4.0 * layers * count * width)

    smem = pl.BlockSpec(memory_space=pltpu.SMEM)
    vmem = pl.BlockSpec(memory_space=pltpu.VMEM)
    hbm = pl.BlockSpec(memory_space=pl.ANY)
    field = (3, layers, width, deep)
    padded = (3, layers, width + PAD, deep)
    final = (field, field, (2, 4, nf, nm, layers, width), (2, nm, nf))
    kept = 4 * (2 * math.prod(padded) + math.prod(final[2])) + 2**16
    dma = pltpu.SemaphoreType.DMA
    held = pl.pallas_call(
        functools.partial(main_kernel, count, scale),
        out_shape=tuple(pltpu.VMEM(shape, F32) for shape in (padded, padded) + final[2:]),
        in_specs=[smem] * 6 + [vmem] + [hbm] * 3,
        out_specs=(vmem,) * 4,
        scratch_shapes=[
            pltpu.VMEM((2, 2, width, deep), F32),
            pltpu.VMEM((2, 2, width, deep), F32),
            pltpu.VMEM((2, width, deep), F32),
            pltpu.VMEM(field, F32),
            pltpu.VMEM(field, F32),
            pltpu.VMEM((4, layers, width, deep), F32),
            pltpu.VMEM((layers, width, deep), jnp.int32),
            pltpu.VMEM((STEPS, 4, 8 * nm, width), F32),
            pltpu.VMEM((8 * nm, layers * 2 * deep), BF16),
            pltpu.VMEM((8, deep), F32),
            pltpu.VMEM((count, 8, deep), F32),
            pltpu.VMEM((2, nf, deep), F32),
            pltpu.SMEM((2, nf, deep), F32),
            dma((5,)),
            dma,
            dma((CHUNKS,)),
            dma((2, CHUNKS)),
            dma((CHUNKS,)),
            dma((2, CHUNKS)),
            dma((count,)),
            dma((count,)),
            pltpu.SemaphoreType.REGULAR((count.bit_length(),)),
        ],
        compiler_params=pltpu.CompilerParams(
            collective_id=0, has_side_effects=True, vmem_limit_bytes=VMEM_BYTES - kept
        ),
    )(
        permittivity,
        pole_frequency,
        pole_damping,
        pole_strength,
        frequencies,
        plane_depth,
        mode_fields,
        *(pltpu.with_memory_space_constraint(a, pltpu.HBM) for a in (electric, magnetic, material)),
    )
    return pl.pallas_call(
        place_kernel,
        out_shape=tuple(jax.ShapeDtypeStruct(shape, F32) for shape in final),
        in_specs=[vmem] * 4,
        out_specs=(hbm,) * 4,
        scratch_shapes=[dma((4,))],
        compiler_params=pltpu.CompilerParams(vmem_limit_bytes=16 * 2**20),
    )(*held)


def solution(mesh):
    in_specs = (
        P(None, "gx", None, None),
        P(None, "gx", None, None),
        P(("member", "gx"), None, None),
        P(),
        P(),
        P(),
        P(),
        P(),
        P(),
        P(None, None, "gx", None),
    )
    out_specs = (
        P(None, ("member", "gx"), None, None),
        P(None, ("member", "gx"), None, None),
        P(None, None, None, None, ("member", "gx"), None),
        P("member", None, None),
    )
    return jax.shard_map(
        on_device, mesh=mesh, in_specs=in_specs, out_specs=out_specs, check_vma=False
    )
```

```python
import functools
import math

import jax
import jax.numpy as jnp
from jax import lax
from jax.experimental import pallas as pl
from jax.experimental.pallas import tpu as pltpu
from jax.sharding import PartitionSpec as P

STEPS = 6
DT = 0.5
CHUNKS = 8
ROWS = 32
PAD = 8
MESH = pl.DeviceIdType.MESH
VMEM_BYTES = 67043328
F32 = jnp.float32
BF16 = jnp.bfloat16


def ahead(value):
    width = value.shape[-1]
    lane = lax.broadcasted_iota(jnp.int32, value.shape, 1)
    return jnp.where(lane == width - 1, 0.0, pltpu.roll(value, width - 1, 1))


def behind(value):
    lane = lax.broadcasted_iota(jnp.int32, value.shape, 1)
    return jnp.where(lane == 0, 0.0, pltpu.roll(value, 1, 1))


def main_kernel(
    count,
    scale,
    perm_ref,
    freq_ref,
    damp_ref,
    strength_ref,
    omega_ref,
    depth_ref,
    mode_ref,
    el_ref,
    ma_ref,
    mat_ref,
    eb,
    hb,
    planes,
    rot,
    inter_ref,
    ge,
    gh,
    ph,
    jb,
    pb,
    coef,
    matb,
    pick,
    modes,
    fixed,
    memory,
    near,
    give_up,
    give_down,
    from_down,
    from_up,
    part,
    gathered,
    in_sem,
    se_sem,
    re_sem,
    sh_sem,
    rh_sem,
    sp_sem,
    rp_sem,
    wt_sem,
    met_sem,
):
    me = lax.axis_index("gx")
    layers, width, deep = mat_ref.shape
    nm, nf = depth_ref.shape[0], omega_ref.shape[0]
    chunk = width // CHUNKS
    has_upper = me < count - 1
    has_lower = me > 0
    top = layers - 1

    barrier = pltpu.get_barrier_semaphore()
    for present, side in ((has_lower, me - 1), (has_upper, me + 1)):

        @pl.when(present)
        def _(side=side):
            pl.semaphore_signal(barrier, inc=1, device_id={"gx": side}, device_id_type=MESH)

    rest = pl.ds(0, top)
    loads = [
        pltpu.make_async_copy(el_ref.at[:, top], eb.at[:, top, pl.ds(0, width)], in_sem.at[0]),
        pltpu.make_async_copy(ma_ref.at[:, top], hb.at[:, top, pl.ds(PAD, width)], in_sem.at[1]),
        pltpu.make_async_copy(mat_ref, matb, in_sem.at[2]),
        pltpu.make_async_copy(
            el_ref.at[:, rest], eb.at[:, rest, pl.ds(0, width)], in_sem.at[3]
        ),
        pltpu.make_async_copy(
            ma_ref.at[:, rest], hb.at[:, rest, pl.ds(PAD, width)], in_sem.at[4]
        ),
    ]
    for load in loads:
        load.start()

    def send_e(c, source, slot):
        rows = pl.ds(c * chunk, chunk)
        return pltpu.make_async_remote_copy(
            src_ref=source.at[pl.ds(1, 2), 0, rows],
            dst_ref=ge.at[slot, :, rows],
            send_sem=se_sem.at[c],
            recv_sem=re_sem.at[slot, c],
            device_id={"gx": me - 1},
            device_id_type=MESH,
        )

    def send_h(c, slot):
        rows = pl.ds(c * chunk, chunk)
        return pltpu.make_async_remote_copy(
            src_ref=ph.at[:, rows],
            dst_ref=gh.at[slot, :, rows],
            send_sem=sh_sem.at[c],
            recv_sem=rh_sem.at[slot, c],
            device_id={"gx": me + 1},
            device_id_type=MESH,
        )

    zero_rows = jnp.zeros((PAD, deep), F32)
    for c in range(3):
        for x in range(layers):
            eb[c, x, pl.ds(width, PAD), :] = zero_rows
            hb[c, x, pl.ds(0, PAD), :] = zero_rows
    part[...] = jnp.zeros_like(part)

    pl.semaphore_wait(barrier, has_lower.astype(jnp.int32) + has_upper.astype(jnp.int32))

    @pl.when(has_lower)
    def _():
        for c in range(CHUNKS):
            send_e(c, el_ref, 0).start()

    @pl.when(~has_upper)
    def _():
        ge[...] = jnp.zeros_like(ge)
        from_up[...] = jnp.zeros_like(from_up)

    @pl.when(~has_lower)
    def _():
        gh[...] = jnp.zeros_like(gh)
        from_down[...] = jnp.zeros_like(from_down)

    def partial_h(y, size):
        here, next_y, spot = pl.ds(y, size), pl.ds(y + 1, size), pl.ds(y + PAD, size)
        ex, ey, ez = eb[0, top, here, :], eb[1, top, here, :], eb[2, top, here, :]
        ex_y = eb[0, top, next_y, :]
        ph[0, here, :] = hb[1, top, spot, :] - DT * ((ahead(ex) - ex) + ez)
        ph[1, here, :] = hb[2, top, spot, :] + DT * (ey + (ex_y - ex))

    loads[0].wait()
    loads[1].wait()
    for c in range(CHUNKS):
        partial_h(c * chunk, chunk)

        @pl.when(has_upper)
        def _(c=c):
            send_h(c, 0).start()

    rows = 8 * nm
    shape = pick.shape
    row = lax.broadcasted_iota(jnp.int32, shape, 0)
    col = lax.broadcasted_iota(jnp.int32, shape, 1)
    spot_of = lax.rem(row, rows)
    wanted = jnp.zeros(shape, jnp.int32)
    for m in range(nm):
        wanted = jnp.where(spot_of // 8 == m, depth_ref[m], wanted)
    wanted = jnp.where(row // rows == 1, wanted - 1, wanted)
    wanted = jnp.where(row // rows == 2, wanted + 1, wanted)
    hit = (row % 8 == col // (2 * deep)) & (col % deep == wanted)
    pick[...] = jnp.where(hit, 1.0, 0.0).astype(BF16)

    for c in range(4):
        for m in range(nm):
            value = mode_ref[3 - c, m]
            value = value if c in (0, 3) else -value
            value = jnp.concatenate([value, jnp.zeros((8 - layers, width), F32)], axis=0)
            modes[c, pl.ds(8 * m, 8), :] = value

    lane = lax.broadcasted_iota(jnp.int32, (nf, deep), 1)
    line = lax.broadcasted_iota(jnp.int32, (nf, deep), 0)
    omega = jnp.zeros((nf, deep), F32)
    for f in range(nf):
        omega = jnp.where(line == f, omega_ref[f], omega)
    late = jnp.where(lane % 4 < 2, 1.0, 0.5)
    phase = ((lane // 4).astype(F32) + late) * DT * omega
    rot[0] = jnp.where(lane < 4 * STEPS, jnp.cos(phase), 0.0)
    rot[1] = jnp.where(lane < 4 * STEPS, -jnp.sin(phase), 0.0)

    kinds = perm_ref.shape[0]
    offset = kinds - freq_ref.shape[0]
    ones = jnp.ones((8, deep), F32)
    tables = []
    for kind in range(kinds):
        if kind < offset:
            g, w2, drive = 0.0 * ones, 0.0 * ones, 0.0 * ones
        else:
            p = kind - offset
            g = damp_ref[p] * ones
            w2 = (freq_ref[p] * ones) * freq_ref[p]
            drive = strength_ref[p] * w2
        divisor = 1.0 + 0.5 * DT * g
        tables.append(
            (
                (1.0 - 0.5 * DT * g) / divisor,
                DT * drive / divisor,
                DT * w2 / divisor,
                DT / (perm_ref[kind] * ones),
            )
        )

    loads[2].wait()
    for x in range(layers):

        def fill(b, carry, x=x):
            rows = pl.ds(pl.multiple_of(b * 8, 8), 8)
            q = matb[x, rows, :]
            for i in range(4):
                value = tables[0][i]
                for kind in range(1, kinds):
                    value = jnp.where(q == kind, tables[kind][i], value)
                coef[i, x, rows, :] = value
            zero = jnp.zeros_like(ones)
            for c in range(3):
                jb[c, x, rows, :] = zero
                pb[c, x, rows, :] = zero
            return carry

        lax.fori_loop(0, width // 8, fill, 0, unroll=2)

    loads[3].wait()
    loads[4].wait()

    lower = jnp.where(has_lower, DT, 0.0)

    def select(value_of, groups, size):
        total = jnp.zeros((groups * rows, size), F32)
        for x in range(layers):
            value = value_of(x)
            high = value.astype(BF16)
            low = (value - high.astype(F32)).astype(BF16)
            total = total + lax.dot_general(
                pick[pl.ds(0, groups * rows), pl.ds(x * 2 * deep, 2 * deep)],
                jnp.concatenate([high, low], axis=1),
                (((1,), (1,)), ((), ())),
                preferred_element_type=F32,
            )
        return total

    for i in range(4):
        fixed[i] = select(lambda x, i=i: coef[i, x], 1, width)
    for c in range(2):
        near[c, pl.ds(0, rows), :] = select(
            lambda x, c=c: eb[c, x, pl.ds(0, width), :], 1, width
        )
    memory[...] = jnp.zeros_like(memory)

    line = lax.broadcasted_iota(jnp.int32, (rows, width), 0) % 8

    def placed(values):
        total = jnp.zeros((rows, width), F32)
        for at, (value, source) in enumerate(values):
            if at != source:
                value = pltpu.roll(value, (at - source) % rows, 0)
            total = jnp.where(line == at, value, total)
        return total

    give_up[...] = placed(
        [(modes[3], top), (fixed[3] * modes[0], top), (fixed[3] * modes[1], top)]
    ).reshape(give_up.shape)
    give_down[...] = placed([(fixed[3] * modes[1], 0)]).reshape(give_down.shape)

    def weights_up():
        return pltpu.make_async_remote_copy(
            src_ref=give_up.at[:, pl.ds(0, 4)],
            dst_ref=from_down.at[:, pl.ds(0, 4)],
            send_sem=wt_sem.at[0],
            recv_sem=wt_sem.at[1],
            device_id={"gx": me + 1},
            device_id_type=MESH,
        )

    def weights_down():
        return pltpu.make_async_remote_copy(
            src_ref=give_down.at[:, pl.ds(0, 4)],
            dst_ref=from_up.at[:, pl.ds(0, 4)],
            send_sem=wt_sem.at[2],
            recv_sem=wt_sem.at[3],
            device_id={"gx": me - 1},
            device_id_type=MESH,
        )

    @pl.when(has_upper)
    def _():
        weights_up().start()

    @pl.when(has_lower)
    def _():
        weights_down().start()

    def update_h(x, y, size):
        here, next_y = pl.ds(y, size), pl.ds(y + 1, size)
        spot = pl.ds(y + PAD, size)
        ex, ey, ez = eb[0, x, here, :], eb[1, x, here, :], eb[2, x, here, :]
        ex_y, ez_y = eb[0, x, next_y, :], eb[2, x, next_y, :]
        hb[0, x, spot, :] -= DT * ((ez_y - ez) - (ahead(ey) - ey))
        if x < top:
            ey_x, ez_x = eb[1, x + 1, here, :], eb[2, x + 1, here, :]
            hb[1, x, spot, :] -= DT * ((ahead(ex) - ex) - (ez_x - ez))
            hb[2, x, spot, :] -= DT * ((ey_x - ey) - (ex_y - ex))

    def finish_h(slot, y, size):
        here, spot = pl.ds(y, size), pl.ds(y + PAD, size)
        hb[1, top, spot, :] = ph[0, here, :] + DT * ge[slot, 1, here, :]
        hb[2, top, spot, :] = ph[1, here, :] - DT * ge[slot, 0, here, :]

    def update_e(x, y, size, slot):
        here = pl.ds(y, size)
        spot, last_y = pl.ds(y + PAD, size), pl.ds(y + PAD - 1, size)
        hx, hy, hz = hb[0, x, spot, :], hb[1, x, spot, :], hb[2, x, spot, :]
        hx_y, hz_y = hb[0, x, last_y, :], hb[2, x, last_y, :]
        if x > 0:
            dz = hz - hb[2, x - 1, spot, :]
            dy = hy - hb[1, x - 1, spot, :]
        else:
            dz = hz - (gh[slot, 1, here, :] - lower * eb[1, 0, here, :])
            dy = hy - (gh[slot, 0, here, :] + lower * eb[2, 0, here, :])
        curl = (
            (hz - hz_y) - (hy - behind(hy)),
            (hx - behind(hx)) - dz,
            dy - (hx - hx_y),
        )
        retain, pulling = coef[0, x, here, :], coef[1, x, here, :]
        spring, step_e = coef[2, x, here, :], coef[3, x, here, :]
        for c in range(3):
            field, polar = eb[c, x, here, :], pb[c, x, here, :]
            current = retain * jb[c, x, here, :] + pulling * field - spring * polar
            jb[c, x, here, :] = current
            pb[c, x, here, :] = polar + DT * current
            eb[c, x, here, :] = field + step_e * (curl[c] - current)

    def sweep(update, xs, c, *args):
        size = min(ROWS, chunk)
        for x in xs:
            for y in range(c * chunk, (c + 1) * chunk, size):
                update(x, y, size, *args)

    def note(n, c, product):
        sums = jnp.sum(product.reshape(nm, 8, product.shape[1]), axis=1)
        value = jnp.sum(sums, axis=1, keepdims=True)
        here = lax.broadcasted_iota(jnp.int32, (nm, deep), 1) == n * 4 + c
        kept = part[pl.ds(0, nm), :]
        part[pl.ds(0, nm), :] = kept + jnp.where(here, value, 0.0)

    def record(n, part_of, buf, base, source, c):
        size = width // 2
        cols = pl.ds(part_of * size, size)
        here = pl.ds(base + part_of * size, size)
        last = isinstance(n, int)
        total = select(lambda x: buf[source, x, here, :], 1 if last else 3, size)
        planes[n, c, :, cols] = total[:rows, :]
        if last:
            return
        note(n, c, total[:rows, :] * modes[c, :, cols])
        if c < 2:
            field = near[c, pl.ds(0, rows), cols]
            polar = memory[1, c, :, cols]
            current = fixed[0, :, cols] * memory[0, c, :, cols]
            current = current + fixed[1, :, cols] * field - fixed[2, :, cols] * polar
            memory[0, c, :, cols] = current
            memory[1, c, :, cols] = polar + DT * current
        near[c, :, cols] = total

    def record_all(n, part_of):
        for c in range(2):
            record(n, part_of, eb, 0, c, c)
            record(n, part_of, hb, PAD, c, 2 + c)
        if isinstance(n, int):
            return

        @pl.when(n == STEPS - 2)
        def _():
            size = width // 2
            cols = pl.ds(part_of * size, size)
            for i, buf, base in ((4, eb, 0), (5, hb, PAD)):
                here = pl.ds(base + part_of * size, size)
                near[i, :, cols] = select(lambda x: buf[2, x, here, :], 3, size)

    def foresee():
        final = STEPS - 1

        def at(i, group):
            return near[i, pl.ds(group * rows, rows), :]

        def above(value):
            return jnp.where(line >= top, 0.0, pltpu.roll(value, rows - 1, 0))

        ex, ex_last, ex_next = at(0, 0), at(0, 1), at(0, 2)
        ey, ey_last, ey_next = at(1, 0), at(1, 1), at(1, 2)
        ez, ez_last = at(4, 0), at(4, 1)
        hx = at(2, 0) - DT * ((ahead(ez) - ez) - (ey_next - ey))
        hx_last = at(2, 1) - DT * ((ahead(ez_last) - ez_last) - (ey - ey_last))
        hy = at(3, 0) - DT * ((ex_next - ex) - (above(ez) - ez))
        hy_last = at(3, 1) - DT * ((ex - ex_last) - (above(ez_last) - ez_last))
        hz = at(5, 0) - DT * ((above(ey) - ey) - (ahead(ex) - ex))
        hz_below = jnp.where(line == 0, -lower * ey, pltpu.roll(hz, 1, 0))
        curl = (
            (hz - behind(hz)) - (hy - hy_last),
            (hx - hx_last) - (hz - hz_below),
        )
        for c, field in enumerate((ex, ey)):
            current = fixed[0] * memory[0, c] + fixed[1] * field - fixed[2] * memory[1, c]
            note(final, c, (field + fixed[3] * (curl[c] - current)) * modes[c])
        note(final, 2, hx * modes[2])
        note(final, 3, hy * modes[3])

        @pl.when(has_upper)
        def _():
            weights_up().wait_send()
            weights_down().wait_recv()

        @pl.when(has_lower)
        def _():
            weights_down().wait_send()
            weights_up().wait_recv()

        def known(ref):
            return jnp.where(line < 4, ref[...].reshape(rows, width), 0.0)

        rise = jnp.where(line == 0, pltpu.roll(hz, rows - top, 0), 0.0)
        note(final, 1, known(from_up) * rise)
        step_x = (ey - behind(ey)) + (ez - ez_last)
        fall = placed([(DT * ez, 0), (-DT * step_x, 0), (DT * ey, 0)]) * known(from_down)
        for at_line, c in enumerate((3, 0, 1)):
            note(final, c, jnp.where(line == at_line, fall, 0.0))

    reach = [d for d in (4 << i for i in range(count.bit_length())) if d < count]

    def greet(i):
        for present, side in ((me >= reach[i], me - reach[i]), (me < count - reach[i], me + reach[i])):

            @pl.when(present)
            def _(side=side):
                pl.semaphore_signal(
                    met_sem.at[i], inc=1, device_id={"gx": side}, device_id_type=MESH
                )

    def met(i):
        peers = sum(p.astype(jnp.int32) for p in (me >= reach[i], me < count - reach[i]))
        pl.semaphore_wait(met_sem.at[i], peers)

    def send_up(n, c, slot):
        @pl.when(has_upper)
        def _():
            send_h(c, slot).wait_send()

        if isinstance(n, int):
            return
        partial_h(c * chunk, chunk)

        @pl.when(has_upper)
        def _():
            send_h(c, slot).start()

    def step(n, carry):
        last = isinstance(n, int)
        slot = n % 2 if last else lax.rem(n, 2)
        other = 1 - slot
        for c in range(CHUNKS):
            sweep(update_h, range(layers), c)

            @pl.when(has_upper)
            def _(c=c):
                send_e(c, eb, slot).wait_recv()

            @pl.when(has_lower)
            def _(c=c):
                send_h(c, slot).wait_recv()
                send_e(c, eb, slot).wait_send()

            finish_h(slot, c * chunk, chunk)
            sweep(update_e, (0, top), c, slot)

            if not last:

                @pl.when(has_lower)
                def _(c=c):
                    send_e(c, eb, other).start()

            if c > 0:
                send_up(n, c - 1, other)
            sweep(update_e, range(1, top), c, slot)
            if c == CHUNKS // 2 - 1:
                record_all(n, 0)
        send_up(n, CHUNKS - 1, other)
        record_all(n, 1)
        if last:
            return carry
        for i in range(min(len(reach), STEPS - 3)):

            @pl.when(n == i + 2)
            def _(i=i):
                if i > 0:
                    met(i - 1)
                greet(i)

        return carry

    lax.fori_loop(0, STEPS - 1, step, 0)
    foresee()

    begun = min(len(reach), STEPS - 3)
    for i in range(max(begun - 1, 0), len(reach)):
        if i >= begun:
            greet(i)
        met(i)

    def share(k, slot):
        return pltpu.make_async_remote_copy(
            src_ref=part,
            dst_ref=gathered.at[slot],
            send_sem=sp_sem.at[k],
            recv_sem=rp_sem.at[k],
            device_id={"gx": lax.rem(me + k, count)},
            device_id_type=MESH,
        )

    for k in range(1, count):
        share(k, me).start()
    gathered[me] = part[...]

    step(STEPS - 1, 0)

    for k in range(1, count):
        share(k, lax.rem(me - k + count, count)).wait()
    full = gathered[0]
    for k in range(1, count):
        full = full + gathered[k]
    for r in range(2):
        out = lax.dot_general(
            full,
            rot[r],
            (((1,), (1,)), ((), ())),
            preferred_element_type=F32,
            precision=lax.Precision.HIGHEST,
        )
        inter_ref[r] = scale * out[:nm, :]


def place_kernel(
    eb, hb, planes, rot, inter, el_out, ma_out, mon_out, inter_out, mon, rot_s, sems, mon_sem
):
    layers, width = el_out.shape[1:3]
    nf, nm = mon.shape[2:4]
    to_scalars = pltpu.make_async_copy(rot, rot_s, sems.at[3])
    to_scalars.start()
    copies = [
        pltpu.make_async_copy(eb.at[:, :, pl.ds(0, width)], el_out, sems.at[0]),
        pltpu.make_async_copy(hb.at[:, :, pl.ds(PAD, width)], ma_out, sems.at[1]),
        pltpu.make_async_copy(inter, inter_out, sems.at[2]),
    ]
    for copy in copies:
        copy.start()
    to_scalars.wait()
    for c in range(4):

        def fold(m, carry, c=c):
            rows = pl.ds(pl.multiple_of(8 * m, 8), layers)
            plane = [planes[n, c, rows, :] for n in range(STEPS)]
            for r in range(2):
                for f in range(nf):
                    value = rot_s[r, f, c] * plane[0]
                    for n in range(1, STEPS):
                        value = value + rot_s[r, f, n * 4 + c] * plane[n]
                    mon[r, c, f, m] = value
            return carry

        lax.fori_loop(0, nm, fold, 0)
        copies.append(pltpu.make_async_copy(mon.at[:, c], mon_out.at[:, c], mon_sem.at[c]))
        copies[-1].start()
    for copy in copies:
        copy.wait()


def on_device(
    electric,
    magnetic,
    material,
    permittivity,
    pole_frequency,
    pole_damping,
    pole_strength,
    frequencies,
    plane_depth,
    mode_fields,
):
    count = lax.axis_size("gx")
    layers, width, deep = material.shape
    nm, nf = plane_depth.shape[0], frequencies.shape[0]
    scale = 1.0 / math.sqrt(4.0 * layers * count * width)

    smem = pl.BlockSpec(memory_space=pltpu.SMEM)
    vmem = pl.BlockSpec(memory_space=pltpu.VMEM)
    hbm = pl.BlockSpec(memory_space=pl.ANY)
    field = (3, layers, width, deep)
    padded = (3, layers, width + PAD, deep)
    final = (field, field, (2, 4, nf, nm, layers, width), (2, nm, nf))
    planar = (8 * nm, width)
    shapes = (padded, padded, (STEPS, 4) + planar, (2, nf, deep), (2, nm, nf))
    kept = 4 * sum(math.prod(shape) for shape in shapes[:3]) + 2**17
    dma = pltpu.SemaphoreType.DMA
    held = pl.pallas_call(
        functools.partial(main_kernel, count, scale),
        out_shape=tuple(pltpu.VMEM(shape, F32) for shape in shapes),
        in_specs=[smem] * 6 + [vmem] + [hbm] * 3,
        out_specs=(vmem,) * 5,
        scratch_shapes=[
            pltpu.VMEM((2, 2, width, deep), F32),
            pltpu.VMEM((2, 2, width, deep), F32),
            pltpu.VMEM((2, width, deep), F32),
            pltpu.VMEM(field, F32),
            pltpu.VMEM(field, F32),
            pltpu.VMEM((4, layers, width, deep), F32),
            pltpu.VMEM((layers, width, deep), jnp.int32),
            pltpu.VMEM((3 * 8 * nm, layers * 2 * deep), BF16),
            pltpu.VMEM((4,) + planar, F32),
            pltpu.VMEM((4,) + planar, F32),
            pltpu.VMEM((2, 2) + planar, F32),
            pltpu.VMEM((6, 3 * 8 * nm, width), F32),
            pltpu.VMEM((nm, 8, width), F32),
            pltpu.VMEM((nm, 8, width), F32),
            pltpu.VMEM((nm, 8, width), F32),
            pltpu.VMEM((nm, 8, width), F32),
            pltpu.VMEM((8, deep), F32),
            pltpu.VMEM((count, 8, deep), F32),
            dma((5,)),
            dma((CHUNKS,)),
            dma((2, CHUNKS)),
            dma((CHUNKS,)),
            dma((2, CHUNKS)),
            dma((count,)),
            dma((count,)),
            dma((4,)),
            pltpu.SemaphoreType.REGULAR((count.bit_length(),)),
        ],
        compiler_params=pltpu.CompilerParams(
            collective_id=0, has_side_effects=True, vmem_limit_bytes=VMEM_BYTES - kept
        ),
    )(
        permittivity,
        pole_frequency,
        pole_damping,
        pole_strength,
        frequencies,
        plane_depth,
        mode_fields,
        *(pltpu.with_memory_space_constraint(a, pltpu.HBM) for a in (electric, magnetic, material)),
    )
    return pl.pallas_call(
        place_kernel,
        out_shape=tuple(jax.ShapeDtypeStruct(shape, F32) for shape in final),
        in_specs=[vmem] * 5,
        out_specs=(hbm,) * 4,
        scratch_shapes=[
            pltpu.VMEM(final[2], F32),
            pltpu.SMEM((2, nf, deep), F32),
            dma((4,)),
            dma((4,)),
        ],
        compiler_params=pltpu.CompilerParams(vmem_limit_bytes=16 * 2**20),
    )(*held)


def solution(mesh):
    in_specs = (
        P(None, "gx", None, None),
        P(None, "gx", None, None),
        P(("member", "gx"), None, None),
        P(),
        P(),
        P(),
        P(),
        P(),
        P(),
        P(None, None, "gx", None),
    )
    out_specs = (
        P(None, ("member", "gx"), None, None),
        P(None, ("member", "gx"), None, None),
        P(None, None, None, None, ("member", "gx"), None),
        P("member", None, None),
    )
    return jax.shard_map(
        on_device, mesh=mesh, in_specs=in_specs, out_specs=out_specs, check_vma=False
    )
```

```python
import functools
import math

import jax
import jax.numpy as jnp
from jax import lax
from jax.experimental import pallas as pl
from jax.experimental.pallas import tpu as pltpu
from jax.sharding import PartitionSpec as P

STEPS = 6
DT = 0.5
CHUNKS = 8
ROWS = 32
PAD = 8
HELD = 3
MESH = pl.DeviceIdType.MESH
VMEM_BYTES = 67043328
F32 = jnp.float32
BF16 = jnp.bfloat16


def ahead(value):
    width = value.shape[-1]
    lane = lax.broadcasted_iota(jnp.int32, value.shape, 1)
    return jnp.where(lane == width - 1, 0.0, pltpu.roll(value, width - 1, 1))


def behind(value):
    lane = lax.broadcasted_iota(jnp.int32, value.shape, 1)
    return jnp.where(lane == 0, 0.0, pltpu.roll(value, 1, 1))


def select(pick, layers, value_of, groups):
    rows, span = pick.shape[0] // 3 * groups, pick.shape[1] // layers
    total = 0.0
    for x in range(layers):
        value = value_of(x)
        high = value.astype(BF16)
        low = (value - high.astype(F32)).astype(BF16)
        total = total + lax.dot_general(
            pick[pl.ds(0, rows), pl.ds(x * span, span)],
            jnp.concatenate([high, low], axis=1),
            (((1,), (1,)), ((), ())),
            preferred_element_type=F32,
        )
    return total


def main_kernel(
    count,
    perm_ref,
    freq_ref,
    damp_ref,
    strength_ref,
    omega_ref,
    depth_ref,
    mode_ref,
    el_ref,
    ma_ref,
    mat_ref,
    eb,
    hb,
    mon,
    rot,
    full,
    ge,
    gh,
    ph,
    jb,
    pb,
    coef,
    matb,
    pick,
    planes,
    modes,
    fixed,
    memory,
    near,
    give_up,
    give_down,
    from_down,
    from_up,
    part,
    gathered,
    rot_s,
    rot_sem,
    in_sem,
    se_sem,
    re_sem,
    sh_sem,
    rh_sem,
    sp_sem,
    rp_sem,
    wt_sem,
    met_sem,
):
    me = lax.axis_index("gx")
    layers, width, deep = mat_ref.shape
    nm, nf = depth_ref.shape[0], omega_ref.shape[0]
    chunk = width // CHUNKS
    has_upper = me < count - 1
    has_lower = me > 0
    top = layers - 1

    barrier = pltpu.get_barrier_semaphore()
    for present, side in ((has_lower, me - 1), (has_upper, me + 1)):

        @pl.when(present)
        def _(side=side):
            pl.semaphore_signal(barrier, inc=1, device_id={"gx": side}, device_id_type=MESH)

    rest = pl.ds(0, top)
    loads = [
        pltpu.make_async_copy(el_ref.at[:, top], eb.at[:, top, pl.ds(0, width)], in_sem.at[0]),
        pltpu.make_async_copy(ma_ref.at[:, top], hb.at[:, top, pl.ds(PAD, width)], in_sem.at[1]),
        pltpu.make_async_copy(mat_ref, matb, in_sem.at[2]),
        pltpu.make_async_copy(
            el_ref.at[:, rest], eb.at[:, rest, pl.ds(0, width)], in_sem.at[3]
        ),
        pltpu.make_async_copy(
            ma_ref.at[:, rest], hb.at[:, rest, pl.ds(PAD, width)], in_sem.at[4]
        ),
    ]
    for load in loads:
        load.start()

    def send_e(c, source, slot):
        rows = pl.ds(c * chunk, chunk)
        return pltpu.make_async_remote_copy(
            src_ref=source.at[pl.ds(1, 2), 0, rows],
            dst_ref=ge.at[slot, :, rows],
            send_sem=se_sem.at[c],
            recv_sem=re_sem.at[slot, c],
            device_id={"gx": me - 1},
            device_id_type=MESH,
        )

    def send_h(c, slot):
        rows = pl.ds(c * chunk, chunk)
        return pltpu.make_async_remote_copy(
            src_ref=ph.at[:, rows],
            dst_ref=gh.at[slot, :, rows],
            send_sem=sh_sem.at[c],
            recv_sem=rh_sem.at[slot, c],
            device_id={"gx": me + 1},
            device_id_type=MESH,
        )

    zero_rows = jnp.zeros((PAD, deep), F32)
    for c in range(3):
        for x in range(layers):
            eb[c, x, pl.ds(width, PAD), :] = zero_rows
            hb[c, x, pl.ds(0, PAD), :] = zero_rows
    part[...] = jnp.zeros_like(part)

    pl.semaphore_wait(barrier, has_lower.astype(jnp.int32) + has_upper.astype(jnp.int32))

    @pl.when(has_lower)
    def _():
        for c in range(CHUNKS):
            send_e(c, el_ref, 0).start()

    @pl.when(~has_upper)
    def _():
        ge[...] = jnp.zeros_like(ge)
        from_up[...] = jnp.zeros_like(from_up)

    @pl.when(~has_lower)
    def _():
        gh[...] = jnp.zeros_like(gh)
        from_down[...] = jnp.zeros_like(from_down)

    def partial_h(y, size):
        here, next_y, spot = pl.ds(y, size), pl.ds(y + 1, size), pl.ds(y + PAD, size)
        ex, ey, ez = eb[0, top, here, :], eb[1, top, here, :], eb[2, top, here, :]
        ex_y = eb[0, top, next_y, :]
        ph[0, here, :] = hb[1, top, spot, :] - DT * ((ahead(ex) - ex) + ez)
        ph[1, here, :] = hb[2, top, spot, :] + DT * (ey + (ex_y - ex))

    loads[0].wait()
    loads[1].wait()
    for c in range(CHUNKS):
        partial_h(c * chunk, chunk)

        @pl.when(has_upper)
        def _(c=c):
            send_h(c, 0).start()

    rows = 8 * nm
    shape = pick.shape
    row = lax.broadcasted_iota(jnp.int32, shape, 0)
    col = lax.broadcasted_iota(jnp.int32, shape, 1)
    spot_of = lax.rem(row, rows)
    wanted = jnp.zeros(shape, jnp.int32)
    for m in range(nm):
        wanted = jnp.where(spot_of // 8 == m, depth_ref[m], wanted)
    wanted = jnp.where(row // rows == 1, wanted - 1, wanted)
    wanted = jnp.where(row // rows == 2, wanted + 1, wanted)
    hit = (row % 8 == col // (2 * deep)) & (col % deep == wanted)
    pick[...] = jnp.where(hit, 1.0, 0.0).astype(BF16)

    for c in range(4):
        for m in range(nm):
            value = mode_ref[3 - c, m]
            value = value if c in (0, 3) else -value
            value = jnp.concatenate([value, jnp.zeros((8 - layers, width), F32)], axis=0)
            modes[c, pl.ds(8 * m, 8), :] = value

    lane = lax.broadcasted_iota(jnp.int32, (nf, deep), 1)
    line = lax.broadcasted_iota(jnp.int32, (nf, deep), 0)
    omega = jnp.zeros((nf, deep), F32)
    for f in range(nf):
        omega = jnp.where(line == f, omega_ref[f], omega)
    late = jnp.where(lane % 4 < 2, 1.0, 0.5)
    phase = ((lane // 4).astype(F32) + late) * DT * omega
    rot[0] = jnp.where(lane < 4 * STEPS, jnp.cos(phase), 0.0)
    rot[1] = jnp.where(lane < 4 * STEPS, -jnp.sin(phase), 0.0)

    kinds = perm_ref.shape[0]
    offset = kinds - freq_ref.shape[0]
    ones = jnp.ones((8, deep), F32)
    tables = []
    for kind in range(kinds):
        if kind < offset:
            g, w2, drive = 0.0 * ones, 0.0 * ones, 0.0 * ones
        else:
            p = kind - offset
            g = damp_ref[p] * ones
            w2 = (freq_ref[p] * ones) * freq_ref[p]
            drive = strength_ref[p] * w2
        divisor = 1.0 + 0.5 * DT * g
        tables.append(
            (
                (1.0 - 0.5 * DT * g) / divisor,
                DT * drive / divisor,
                DT * w2 / divisor,
                DT / (perm_ref[kind] * ones),
            )
        )

    loads[2].wait()
    for x in range(layers):

        def fill(b, carry, x=x):
            rows = pl.ds(pl.multiple_of(b * 8, 8), 8)
            q = matb[x, rows, :]
            for i in range(4):
                value = tables[0][i]
                for kind in range(1, kinds):
                    value = jnp.where(q == kind, tables[kind][i], value)
                coef[i, x, rows, :] = value
            zero = jnp.zeros_like(ones)
            for c in range(3):
                jb[c, x, rows, :] = zero
                pb[c, x, rows, :] = zero
            return carry

        lax.fori_loop(0, width // 8, fill, 0, unroll=2)

    loads[3].wait()
    loads[4].wait()

    lower = jnp.where(has_lower, DT, 0.0)

    for i in range(4):
        fixed[i] = select(pick, layers, lambda x, i=i: coef[i, x], 1)
    for c in range(2):
        near[c, pl.ds(0, rows), :] = select(
            pick, layers, lambda x, c=c: eb[c, x, pl.ds(0, width), :], 1
        )
    memory[...] = jnp.zeros_like(memory)

    line = lax.broadcasted_iota(jnp.int32, (rows, width), 0) % 8

    def placed(values):
        total = jnp.zeros((rows, width), F32)
        for at, (value, source) in enumerate(values):
            if at != source:
                value = pltpu.roll(value, (at - source) % rows, 0)
            total = jnp.where(line == at, value, total)
        return total

    give_up[...] = placed(
        [(modes[3], top), (fixed[3] * modes[0], top), (fixed[3] * modes[1], top)]
    ).reshape(give_up.shape)
    give_down[...] = placed([(fixed[3] * modes[1], 0)]).reshape(give_down.shape)

    def weights_up():
        return pltpu.make_async_remote_copy(
            src_ref=give_up.at[:, pl.ds(0, 4)],
            dst_ref=from_down.at[:, pl.ds(0, 4)],
            send_sem=wt_sem.at[0],
            recv_sem=wt_sem.at[1],
            device_id={"gx": me + 1},
            device_id_type=MESH,
        )

    def weights_down():
        return pltpu.make_async_remote_copy(
            src_ref=give_down.at[:, pl.ds(0, 4)],
            dst_ref=from_up.at[:, pl.ds(0, 4)],
            send_sem=wt_sem.at[2],
            recv_sem=wt_sem.at[3],
            device_id={"gx": me - 1},
            device_id_type=MESH,
        )

    @pl.when(has_upper)
    def _():
        weights_up().start()

    @pl.when(has_lower)
    def _():
        weights_down().start()

    def update_h(x, y, size):
        here, next_y = pl.ds(y, size), pl.ds(y + 1, size)
        spot = pl.ds(y + PAD, size)
        ex, ey, ez = eb[0, x, here, :], eb[1, x, here, :], eb[2, x, here, :]
        ex_y, ez_y = eb[0, x, next_y, :], eb[2, x, next_y, :]
        hb[0, x, spot, :] -= DT * ((ez_y - ez) - (ahead(ey) - ey))
        if x < top:
            ey_x, ez_x = eb[1, x + 1, here, :], eb[2, x + 1, here, :]
            hb[1, x, spot, :] -= DT * ((ahead(ex) - ex) - (ez_x - ez))
            hb[2, x, spot, :] -= DT * ((ey_x - ey) - (ex_y - ex))

    def finish_h(slot, y, size):
        here, spot = pl.ds(y, size), pl.ds(y + PAD, size)
        hb[1, top, spot, :] = ph[0, here, :] + DT * ge[slot, 1, here, :]
        hb[2, top, spot, :] = ph[1, here, :] - DT * ge[slot, 0, here, :]

    def update_e(x, y, size, slot):
        here = pl.ds(y, size)
        spot, last_y = pl.ds(y + PAD, size), pl.ds(y + PAD - 1, size)
        hx, hy, hz = hb[0, x, spot, :], hb[1, x, spot, :], hb[2, x, spot, :]
        hx_y, hz_y = hb[0, x, last_y, :], hb[2, x, last_y, :]
        if x > 0:
            dz = hz - hb[2, x - 1, spot, :]
            dy = hy - hb[1, x - 1, spot, :]
        else:
            dz = hz - (gh[slot, 1, here, :] - lower * eb[1, 0, here, :])
            dy = hy - (gh[slot, 0, here, :] + lower * eb[2, 0, here, :])
        curl = (
            (hz - hz_y) - (hy - behind(hy)),
            (hx - behind(hx)) - dz,
            dy - (hx - hx_y),
        )
        retain, pulling = coef[0, x, here, :], coef[1, x, here, :]
        spring, step_e = coef[2, x, here, :], coef[3, x, here, :]
        for c in range(3):
            field, polar = eb[c, x, here, :], pb[c, x, here, :]
            current = retain * jb[c, x, here, :] + pulling * field - spring * polar
            jb[c, x, here, :] = current
            pb[c, x, here, :] = polar + DT * current
            eb[c, x, here, :] = field + step_e * (curl[c] - current)

    def sweep(update, xs, c, *args):
        size = min(ROWS, chunk)
        for x in xs:
            for y in range(c * chunk, (c + 1) * chunk, size):
                update(x, y, size, *args)

    def note(n, c, product):
        sums = jnp.sum(product.reshape(nm, 8, product.shape[1]), axis=1)
        value = jnp.sum(sums, axis=1, keepdims=True)
        here = lax.broadcasted_iota(jnp.int32, (nm, deep), 1) == n * 4 + c
        kept = part[pl.ds(0, nm), :]
        part[pl.ds(0, nm), :] = kept + jnp.where(here, value, 0.0)

    def record(n, part_of, buf, base, source, c):
        size = width // 2
        cols = pl.ds(part_of * size, size)
        here = pl.ds(base + part_of * size, size)
        last = isinstance(n, int)
        total = select(pick, layers, lambda x: buf[source, x, here, :], 1 if last else 3)
        planes[n, c, :, cols] = total[:rows, :]
        if last:
            return
        note(n, c, total[:rows, :] * modes[c, :, cols])
        if c < 2:
            field = near[c, pl.ds(0, rows), cols]
            polar = memory[1, c, :, cols]
            current = fixed[0, :, cols] * memory[0, c, :, cols]
            current = current + fixed[1, :, cols] * field - fixed[2, :, cols] * polar
            memory[0, c, :, cols] = current
            memory[1, c, :, cols] = polar + DT * current
        near[c, :, cols] = total

    def record_all(n, part_of):
        for c in range(2):
            record(n, part_of, eb, 0, c, c)
            record(n, part_of, hb, PAD, c, 2 + c)
        if isinstance(n, int):
            return

        @pl.when(n == STEPS - 2)
        def _():
            size = width // 2
            cols = pl.ds(part_of * size, size)
            for i, buf, base in ((4, eb, 0), (5, hb, PAD)):
                here = pl.ds(base + part_of * size, size)
                near[i, :, cols] = select(pick, layers, lambda x: buf[2, x, here, :], 3)

    def foresee():
        final = STEPS - 1

        def at(i, group):
            return near[i, pl.ds(group * rows, rows), :]

        def above(value):
            return jnp.where(line >= top, 0.0, pltpu.roll(value, rows - 1, 0))

        ex, ex_last, ex_next = at(0, 0), at(0, 1), at(0, 2)
        ey, ey_last, ey_next = at(1, 0), at(1, 1), at(1, 2)
        ez, ez_last = at(4, 0), at(4, 1)
        hx = at(2, 0) - DT * ((ahead(ez) - ez) - (ey_next - ey))
        hx_last = at(2, 1) - DT * ((ahead(ez_last) - ez_last) - (ey - ey_last))
        hy = at(3, 0) - DT * ((ex_next - ex) - (above(ez) - ez))
        hy_last = at(3, 1) - DT * ((ex - ex_last) - (above(ez_last) - ez_last))
        hz = at(5, 0) - DT * ((above(ey) - ey) - (ahead(ex) - ex))
        hz_below = jnp.where(line == 0, -lower * ey, pltpu.roll(hz, 1, 0))
        curl = (
            (hz - behind(hz)) - (hy - hy_last),
            (hx - hx_last) - (hz - hz_below),
        )
        for c, field in enumerate((ex, ey)):
            current = fixed[0] * memory[0, c] + fixed[1] * field - fixed[2] * memory[1, c]
            note(final, c, (field + fixed[3] * (curl[c] - current)) * modes[c])
        note(final, 2, hx * modes[2])
        note(final, 3, hy * modes[3])

        @pl.when(has_upper)
        def _():
            weights_up().wait_send()
            weights_down().wait_recv()

        @pl.when(has_lower)
        def _():
            weights_down().wait_send()
            weights_up().wait_recv()

        def known(ref):
            return jnp.where(line < 4, ref[...].reshape(rows, width), 0.0)

        rise = jnp.where(line == 0, pltpu.roll(hz, rows - top, 0), 0.0)
        note(final, 1, known(from_up) * rise)
        step_x = (ey - behind(ey)) + (ez - ez_last)
        fall = placed([(DT * ez, 0), (-DT * step_x, 0), (DT * ey, 0)]) * known(from_down)
        for at_line, c in enumerate((3, 0, 1)):
            note(final, c, jnp.where(line == at_line, fall, 0.0))

    reach = [d for d in (4 << i for i in range(count.bit_length())) if d < count]

    def greet(i):
        for present, side in ((me >= reach[i], me - reach[i]), (me < count - reach[i], me + reach[i])):

            @pl.when(present)
            def _(side=side):
                pl.semaphore_signal(
                    met_sem.at[i], inc=1, device_id={"gx": side}, device_id_type=MESH
                )

    def met(i):
        peers = sum(p.astype(jnp.int32) for p in (me >= reach[i], me < count - reach[i]))
        pl.semaphore_wait(met_sem.at[i], peers)

    def due(n, c):
        return (n < STEPS - 2) | (c < CHUNKS - HELD)

    def send_up(n, c, slot):
        @pl.when(has_upper)
        def _():
            send_h(c, slot).wait_send()

        if isinstance(n, int):
            return
        partial_h(c * chunk, chunk)

        @pl.when(has_upper & due(n, c))
        def _():
            send_h(c, slot).start()

    to_scalars = pltpu.make_async_copy(rot, rot_s, rot_sem)
    to_scalars.start()

    def fold():
        to_scalars.wait()
        for c in range(4):

            def body(m, carry, c=c):
                here = pl.ds(pl.multiple_of(8 * m, 8), layers)
                plane = [planes[n, c, here, :] for n in range(STEPS)]
                for r in range(2):
                    for f in range(nf):
                        value = rot_s[r, f, c] * plane[0]
                        for n in range(1, STEPS):
                            value = value + rot_s[r, f, n * 4 + c] * plane[n]
                        mon[r, c, f, m] = value
                return carry

            lax.fori_loop(0, nm, body, 0)

    def step(n, carry):
        last = isinstance(n, int)
        slot = n % 2 if last else lax.rem(n, 2)
        other = 1 - slot
        for c in range(CHUNKS):
            sweep(update_h, range(layers), c)

            @pl.when(has_upper)
            def _(c=c):
                send_e(c, eb, slot).wait_recv()

            @pl.when(has_lower)
            def _(c=c):
                send_h(c, slot).wait_recv()
                send_e(c, eb, slot).wait_send()

            finish_h(slot, c * chunk, chunk)
            sweep(update_e, (0, top), c, slot)

            if not last:

                @pl.when(has_lower & due(n, c))
                def _(c=c):
                    send_e(c, eb, other).start()

            if c > 0:
                send_up(n, c - 1, other)
            sweep(update_e, range(1, top), c, slot)
            if c == CHUNKS // 2 - 1:
                record_all(n, 0)
        send_up(n, CHUNKS - 1, other)
        record_all(n, 1)
        if last:
            return carry
        for i in range(min(len(reach), STEPS - 3)):

            @pl.when(n == i + 2)
            def _(i=i):
                if i > 0:
                    met(i - 1)
                greet(i)

        return carry

    lax.fori_loop(0, STEPS - 1, step, 0)
    foresee()

    begun = min(len(reach), STEPS - 3)
    for i in range(max(begun - 1, 0), len(reach)):
        if i >= begun:
            greet(i)
        met(i)

    def share(k, slot):
        return pltpu.make_async_remote_copy(
            src_ref=part,
            dst_ref=gathered.at[slot],
            send_sem=sp_sem,
            recv_sem=rp_sem,
            device_id={"gx": lax.rem(me + k, count)},
            device_id_type=MESH,
        )

    for k in range(1, count):
        share(k, me).start()
    for c in range(CHUNKS - HELD, CHUNKS):

        @pl.when(has_upper)
        def _(c=c):
            send_h(c, (STEPS - 1) % 2).start()

        @pl.when(has_lower)
        def _(c=c):
            send_e(c, eb, (STEPS - 1) % 2).start()

    gathered[me] = part[...]

    step(STEPS - 1, 0)
    fold()

    others = gathered.at[pl.ds(0, count - 1)]
    arrivals = pltpu.make_async_remote_copy(
        src_ref=others,
        dst_ref=others,
        send_sem=sp_sem,
        recv_sem=rp_sem,
        device_id={"gx": lax.rem(me + 1, count)},
        device_id_type=MESH,
    )
    arrivals.wait_send()
    arrivals.wait_recv()
    total = gathered[0]
    for k in range(1, count):
        total = total + gathered[k]
    full[...] = total


def place_kernel(
    scale, eb, hb, mon, rot, full, el_out, ma_out, mon_out, inter_out, inter, sems
):
    width, nm = el_out.shape[2], mon.shape[3]
    copies = [
        pltpu.make_async_copy(eb.at[:, :, pl.ds(0, width)], el_out, sems.at[0]),
        pltpu.make_async_copy(hb.at[:, :, pl.ds(PAD, width)], ma_out, sems.at[1]),
        pltpu.make_async_copy(mon, mon_out, sems.at[2]),
        pltpu.make_async_copy(inter, inter_out, sems.at[3]),
    ]
    for copy in copies[:3]:
        copy.start()
    for r in range(2):
        out = lax.dot_general(
            full[...],
            rot[r],
            (((1,), (1,)), ((), ())),
            preferred_element_type=F32,
            precision=lax.Precision.HIGHEST,
        )
        inter[r] = scale * out[:nm, :]
    copies[3].start()
    for copy in copies:
        copy.wait()


def on_device(
    electric,
    magnetic,
    material,
    permittivity,
    pole_frequency,
    pole_damping,
    pole_strength,
    frequencies,
    plane_depth,
    mode_fields,
):
    count = lax.axis_size("gx")
    layers, width, deep = material.shape
    nm, nf = plane_depth.shape[0], frequencies.shape[0]
    scale = 1.0 / math.sqrt(4.0 * layers * count * width)

    smem = pl.BlockSpec(memory_space=pltpu.SMEM)
    vmem = pl.BlockSpec(memory_space=pltpu.VMEM)
    hbm = pl.BlockSpec(memory_space=pl.ANY)
    field = (3, layers, width, deep)
    padded = (3, layers, width + PAD, deep)
    final = (field, field, (2, 4, nf, nm, layers, width), (2, nm, nf))
    planar = (8 * nm, width)
    shapes = (padded, padded, final[2], (2, nf, deep), (8, deep))
    kept = 4 * sum(math.prod(shape) for shape in shapes[:3]) + 2**17
    dma = pltpu.SemaphoreType.DMA
    held = pl.pallas_call(
        functools.partial(main_kernel, count),
        out_shape=tuple(pltpu.VMEM(shape, F32) for shape in shapes),
        in_specs=[smem] * 6 + [vmem] + [hbm] * 3,
        out_specs=(vmem,) * 5,
        scratch_shapes=[
            pltpu.VMEM((2, 2, width, deep), F32),
            pltpu.VMEM((2, 2, width, deep), F32),
            pltpu.VMEM((2, width, deep), F32),
            pltpu.VMEM(field, F32),
            pltpu.VMEM(field, F32),
            pltpu.VMEM((4, layers, width, deep), F32),
            pltpu.VMEM((layers, width, deep), jnp.int32),
            pltpu.VMEM((3 * 8 * nm, layers * 2 * deep), BF16),
            pltpu.VMEM((STEPS, 4) + planar, F32),
            pltpu.VMEM((4,) + planar, F32),
            pltpu.VMEM((4,) + planar, F32),
            pltpu.VMEM((2, 2) + planar, F32),
            pltpu.VMEM((6, 3 * 8 * nm, width), F32),
            pltpu.VMEM((nm, 8, width), F32),
            pltpu.VMEM((nm, 8, width), F32),
            pltpu.VMEM((nm, 8, width), F32),
            pltpu.VMEM((nm, 8, width), F32),
            pltpu.VMEM((8, deep), F32),
            pltpu.VMEM((count, 8, deep), F32),
            pltpu.SMEM((2, nf, deep), F32),
            dma,
            dma((5,)),
            dma((CHUNKS,)),
            dma((2, CHUNKS)),
            dma((CHUNKS,)),
            dma((2, CHUNKS)),
            dma,
            dma,
            dma((4,)),
            pltpu.SemaphoreType.REGULAR((count.bit_length(),)),
        ],
        compiler_params=pltpu.CompilerParams(
            collective_id=0, has_side_effects=True, vmem_limit_bytes=VMEM_BYTES - kept
        ),
    )(
        permittivity,
        pole_frequency,
        pole_damping,
        pole_strength,
        frequencies,
        plane_depth,
        mode_fields,
        *(pltpu.with_memory_space_constraint(a, pltpu.HBM) for a in (electric, magnetic, material)),
    )
    return pl.pallas_call(
        functools.partial(place_kernel, scale),
        out_shape=tuple(jax.ShapeDtypeStruct(shape, F32) for shape in final),
        in_specs=[vmem] * 5,
        out_specs=(hbm,) * 4,
        scratch_shapes=[
            pltpu.VMEM(final[3], F32),
            dma((4,)),
        ],
        compiler_params=pltpu.CompilerParams(vmem_limit_bytes=16 * 2**20),
    )(*held)


def solution(mesh):
    in_specs = (
        P(None, "gx", None, None),
        P(None, "gx", None, None),
        P(("member", "gx"), None, None),
        P(),
        P(),
        P(),
        P(),
        P(),
        P(),
        P(None, None, "gx", None),
    )
    out_specs = (
        P(None, ("member", "gx"), None, None),
        P(None, ("member", "gx"), None, None),
        P(None, None, None, None, ("member", "gx"), None),
        P("member", None, None),
    )
    return jax.shard_map(
        on_device, mesh=mesh, in_specs=in_specs, out_specs=out_specs, check_vma=False
    )
```

```python
import functools
import math

import jax
import jax.numpy as jnp
from jax import lax
from jax.experimental import pallas as pl
from jax.experimental.pallas import tpu as pltpu
from jax.sharding import PartitionSpec as P

STEPS = 6
DT = 0.5
CHUNKS = 8
ROWS = 32
PAD = 8
HELD = 3
FOLD = 4
MESH = pl.DeviceIdType.MESH
VMEM_BYTES = 67043328
F32 = jnp.float32
BF16 = jnp.bfloat16


def ahead(value):
    width = value.shape[-1]
    lane = lax.broadcasted_iota(jnp.int32, value.shape, 1)
    return jnp.where(lane == width - 1, 0.0, pltpu.roll(value, width - 1, 1))


def behind(value):
    lane = lax.broadcasted_iota(jnp.int32, value.shape, 1)
    return jnp.where(lane == 0, 0.0, pltpu.roll(value, 1, 1))


def select(pick, layers, value_of, groups):
    rows, span = pick.shape[0] // 3 * groups, pick.shape[1] // layers
    total = 0.0
    for x in range(layers):
        value = value_of(x)
        high = value.astype(BF16)
        low = (value - high.astype(F32)).astype(BF16)
        total = total + lax.dot_general(
            pick[pl.ds(0, rows), pl.ds(x * span, span)],
            jnp.concatenate([high, low], axis=1),
            (((1,), (1,)), ((), ())),
            preferred_element_type=F32,
        )
    return total


def main_kernel(
    count,
    perm_ref,
    freq_ref,
    damp_ref,
    strength_ref,
    omega_ref,
    depth_ref,
    mode_ref,
    el_ref,
    ma_ref,
    mat_ref,
    eb,
    hb,
    mon,
    rot,
    full,
    ge,
    gh,
    ph,
    jb,
    pb,
    coef,
    matb,
    pick,
    planes,
    modes,
    fixed,
    memory,
    near,
    give_up,
    give_down,
    from_down,
    from_up,
    part,
    gathered,
    rot_s,
    rot_sem,
    in_sem,
    se_sem,
    re_sem,
    sh_sem,
    rh_sem,
    sp_sem,
    rp_sem,
    wt_sem,
    met_sem,
):
    me = lax.axis_index("gx")
    layers, width, deep = mat_ref.shape
    nm, nf = depth_ref.shape[0], omega_ref.shape[0]
    chunk = width // CHUNKS
    has_upper = me < count - 1
    has_lower = me > 0
    top = layers - 1

    barrier = pltpu.get_barrier_semaphore()
    for present, side in ((has_lower, me - 1), (has_upper, me + 1)):

        @pl.when(present)
        def _(side=side):
            pl.semaphore_signal(barrier, inc=1, device_id={"gx": side}, device_id_type=MESH)

    rest = pl.ds(0, top)
    loads = [
        pltpu.make_async_copy(el_ref.at[:, top], eb.at[:, top, pl.ds(0, width)], in_sem.at[0]),
        pltpu.make_async_copy(ma_ref.at[:, top], hb.at[:, top, pl.ds(PAD, width)], in_sem.at[1]),
        pltpu.make_async_copy(mat_ref, matb, in_sem.at[2]),
        pltpu.make_async_copy(
            el_ref.at[:, rest], eb.at[:, rest, pl.ds(0, width)], in_sem.at[3]
        ),
        pltpu.make_async_copy(
            ma_ref.at[:, rest], hb.at[:, rest, pl.ds(PAD, width)], in_sem.at[4]
        ),
    ]
    for load in loads:
        load.start()

    def send_e(c, source, slot):
        rows = pl.ds(c * chunk, chunk)
        return pltpu.make_async_remote_copy(
            src_ref=source.at[pl.ds(1, 2), 0, rows],
            dst_ref=ge.at[slot, :, rows],
            send_sem=se_sem.at[c],
            recv_sem=re_sem.at[slot, c],
            device_id={"gx": me - 1},
            device_id_type=MESH,
        )

    def send_h(c, slot):
        rows = pl.ds(c * chunk, chunk)
        return pltpu.make_async_remote_copy(
            src_ref=ph.at[:, rows],
            dst_ref=gh.at[slot, :, rows],
            send_sem=sh_sem.at[c],
            recv_sem=rh_sem.at[slot, c],
            device_id={"gx": me + 1},
            device_id_type=MESH,
        )

    zero_rows = jnp.zeros((PAD, deep), F32)
    for c in range(3):
        for x in range(layers):
            eb[c, x, pl.ds(width, PAD), :] = zero_rows
            hb[c, x, pl.ds(0, PAD), :] = zero_rows
    part[...] = jnp.zeros_like(part)

    pl.semaphore_wait(barrier, has_lower.astype(jnp.int32) + has_upper.astype(jnp.int32))

    @pl.when(has_lower)
    def _():
        for c in range(CHUNKS):
            send_e(c, el_ref, 0).start()

    @pl.when(~has_upper)
    def _():
        ge[...] = jnp.zeros_like(ge)
        from_up[...] = jnp.zeros_like(from_up)

    @pl.when(~has_lower)
    def _():
        gh[...] = jnp.zeros_like(gh)
        from_down[...] = jnp.zeros_like(from_down)

    def partial_h(y, size):
        here, next_y, spot = pl.ds(y, size), pl.ds(y + 1, size), pl.ds(y + PAD, size)
        ex, ey, ez = eb[0, top, here, :], eb[1, top, here, :], eb[2, top, here, :]
        ex_y = eb[0, top, next_y, :]
        ph[0, here, :] = hb[1, top, spot, :] - DT * ((ahead(ex) - ex) + ez)
        ph[1, here, :] = hb[2, top, spot, :] + DT * (ey + (ex_y - ex))

    loads[0].wait()
    loads[1].wait()
    for c in range(CHUNKS):
        partial_h(c * chunk, chunk)

        @pl.when(has_upper)
        def _(c=c):
            send_h(c, 0).start()

    rows = 8 * nm
    shape = pick.shape
    row = lax.broadcasted_iota(jnp.int32, shape, 0)
    col = lax.broadcasted_iota(jnp.int32, shape, 1)
    spot_of = lax.rem(row, rows)
    wanted = jnp.zeros(shape, jnp.int32)
    for m in range(nm):
        wanted = jnp.where(spot_of // 8 == m, depth_ref[m], wanted)
    wanted = jnp.where(row // rows == 1, wanted - 1, wanted)
    wanted = jnp.where(row // rows == 2, wanted + 1, wanted)
    hit = (row % 8 == col // (2 * deep)) & (col % deep == wanted)
    pick[...] = jnp.where(hit, 1.0, 0.0).astype(BF16)

    for c in range(4):
        for m in range(nm):
            value = mode_ref[3 - c, m]
            value = value if c in (0, 3) else -value
            value = jnp.concatenate([value, jnp.zeros((8 - layers, width), F32)], axis=0)
            modes[c, pl.ds(8 * m, 8), :] = value

    lane = lax.broadcasted_iota(jnp.int32, (nf, deep), 1)
    line = lax.broadcasted_iota(jnp.int32, (nf, deep), 0)
    omega = jnp.zeros((nf, deep), F32)
    for f in range(nf):
        omega = jnp.where(line == f, omega_ref[f], omega)
    late = jnp.where(lane % 4 < 2, 1.0, 0.5)
    phase = ((lane // 4).astype(F32) + late) * DT * omega
    rot[0] = jnp.where(lane < 4 * STEPS, jnp.cos(phase), 0.0)
    rot[1] = jnp.where(lane < 4 * STEPS, -jnp.sin(phase), 0.0)

    kinds = perm_ref.shape[0]
    offset = kinds - freq_ref.shape[0]
    ones = jnp.ones((8, deep), F32)
    tables = []
    for kind in range(kinds):
        if kind < offset:
            g, w2, drive = 0.0 * ones, 0.0 * ones, 0.0 * ones
        else:
            p = kind - offset
            g = damp_ref[p] * ones
            w2 = (freq_ref[p] * ones) * freq_ref[p]
            drive = strength_ref[p] * w2
        divisor = 1.0 + 0.5 * DT * g
        tables.append(
            (
                (1.0 - 0.5 * DT * g) / divisor,
                DT * drive / divisor,
                DT * w2 / divisor,
                DT / (perm_ref[kind] * ones),
            )
        )

    loads[2].wait()
    for x in range(layers):

        def fill(b, carry, x=x):
            rows = pl.ds(pl.multiple_of(b * 8, 8), 8)
            q = matb[x, rows, :]
            for i in range(4):
                value = tables[0][i]
                for kind in range(1, kinds):
                    value = jnp.where(q == kind, tables[kind][i], value)
                coef[i, x, rows, :] = value
            zero = jnp.zeros_like(ones)
            for c in range(3):
                jb[c, x, rows, :] = zero
                pb[c, x, rows, :] = zero
            return carry

        lax.fori_loop(0, width // 8, fill, 0, unroll=2)

    loads[3].wait()
    loads[4].wait()

    lower = jnp.where(has_lower, DT, 0.0)

    for i in range(4):
        fixed[i] = select(pick, layers, lambda x, i=i: coef[i, x], 1)
    for c in range(2):
        near[c, pl.ds(0, rows), :] = select(
            pick, layers, lambda x, c=c: eb[c, x, pl.ds(0, width), :], 1
        )
    memory[...] = jnp.zeros_like(memory)

    line = lax.broadcasted_iota(jnp.int32, (rows, width), 0) % 8

    def placed(values):
        total = jnp.zeros((rows, width), F32)
        for at, (value, source) in enumerate(values):
            if at != source:
                value = pltpu.roll(value, (at - source) % rows, 0)
            total = jnp.where(line == at, value, total)
        return total

    give_up[...] = placed(
        [(modes[3], top), (fixed[3] * modes[0], top), (fixed[3] * modes[1], top)]
    ).reshape(give_up.shape)
    give_down[...] = placed([(fixed[3] * modes[1], 0)]).reshape(give_down.shape)

    def weights_up():
        return pltpu.make_async_remote_copy(
            src_ref=give_up.at[:, pl.ds(0, 4)],
            dst_ref=from_down.at[:, pl.ds(0, 4)],
            send_sem=wt_sem.at[0],
            recv_sem=wt_sem.at[1],
            device_id={"gx": me + 1},
            device_id_type=MESH,
        )

    def weights_down():
        return pltpu.make_async_remote_copy(
            src_ref=give_down.at[:, pl.ds(0, 4)],
            dst_ref=from_up.at[:, pl.ds(0, 4)],
            send_sem=wt_sem.at[2],
            recv_sem=wt_sem.at[3],
            device_id={"gx": me - 1},
            device_id_type=MESH,
        )

    @pl.when(has_upper)
    def _():
        weights_up().start()

    @pl.when(has_lower)
    def _():
        weights_down().start()

    def update_h(x, y, size):
        here, next_y = pl.ds(y, size), pl.ds(y + 1, size)
        spot = pl.ds(y + PAD, size)
        ex, ey, ez = eb[0, x, here, :], eb[1, x, here, :], eb[2, x, here, :]
        ex_y, ez_y = eb[0, x, next_y, :], eb[2, x, next_y, :]
        hb[0, x, spot, :] -= DT * ((ez_y - ez) - (ahead(ey) - ey))
        if x < top:
            ey_x, ez_x = eb[1, x + 1, here, :], eb[2, x + 1, here, :]
            hb[1, x, spot, :] -= DT * ((ahead(ex) - ex) - (ez_x - ez))
            hb[2, x, spot, :] -= DT * ((ey_x - ey) - (ex_y - ex))

    def finish_h(slot, y, size):
        here, spot = pl.ds(y, size), pl.ds(y + PAD, size)
        hb[1, top, spot, :] = ph[0, here, :] + DT * ge[slot, 1, here, :]
        hb[2, top, spot, :] = ph[1, here, :] - DT * ge[slot, 0, here, :]

    def update_e(x, y, size, slot):
        here = pl.ds(y, size)
        spot, last_y = pl.ds(y + PAD, size), pl.ds(y + PAD - 1, size)
        hx, hy, hz = hb[0, x, spot, :], hb[1, x, spot, :], hb[2, x, spot, :]
        hx_y, hz_y = hb[0, x, last_y, :], hb[2, x, last_y, :]
        if x > 0:
            dz = hz - hb[2, x - 1, spot, :]
            dy = hy - hb[1, x - 1, spot, :]
        else:
            dz = hz - (gh[slot, 1, here, :] - lower * eb[1, 0, here, :])
            dy = hy - (gh[slot, 0, here, :] + lower * eb[2, 0, here, :])
        curl = (
            (hz - hz_y) - (hy - behind(hy)),
            (hx - behind(hx)) - dz,
            dy - (hx - hx_y),
        )
        retain, pulling = coef[0, x, here, :], coef[1, x, here, :]
        spring, step_e = coef[2, x, here, :], coef[3, x, here, :]
        for c in range(3):
            field, polar = eb[c, x, here, :], pb[c, x, here, :]
            current = retain * jb[c, x, here, :] + pulling * field - spring * polar
            jb[c, x, here, :] = current
            pb[c, x, here, :] = polar + DT * current
            eb[c, x, here, :] = field + step_e * (curl[c] - current)

    def sweep(update, xs, c, *args):
        size = min(ROWS, chunk)
        for x in xs:
            for y in range(c * chunk, (c + 1) * chunk, size):
                update(x, y, size, *args)

    def note(n, c, product):
        while product.shape[1] > deep:
            half = product.shape[1] // 2
            product = product[:, :half] + product[:, half:]
        sums = jnp.sum(product.reshape(nm, 8, product.shape[1]), axis=1)
        value = jnp.sum(sums, axis=1, keepdims=True)
        here = lax.broadcasted_iota(jnp.int32, (nm, deep), 1) == n * 4 + c
        return jnp.where(here, value, 0.0)

    def record(n, part_of, buf, base, source, c):
        size = width // 2
        cols = pl.ds(part_of * size, size)
        here = pl.ds(base + part_of * size, size)
        last = isinstance(n, int)
        total = select(pick, layers, lambda x: buf[source, x, here, :], 1 if last else 3)
        planes[n, c, :, cols] = total[:rows, :]
        if last:
            return 0.0
        if c < 2:
            field = near[c, pl.ds(0, rows), cols]
            polar = memory[1, c, :, cols]
            current = fixed[0, :, cols] * memory[0, c, :, cols]
            current = current + fixed[1, :, cols] * field - fixed[2, :, cols] * polar
            memory[0, c, :, cols] = current
            memory[1, c, :, cols] = polar + DT * current
        near[c, :, cols] = total
        return note(n, c, total[:rows, :] * modes[c, :, cols])

    def record_all(n, part_of):
        noted = 0.0
        for c in range(2):
            noted = noted + record(n, part_of, eb, 0, c, c)
            noted = noted + record(n, part_of, hb, PAD, c, 2 + c)
        if isinstance(n, int):
            return
        part[...] += noted

        @pl.when(n == STEPS - 2)
        def _():
            size = width // 2
            cols = pl.ds(part_of * size, size)
            for i, buf, base in ((4, eb, 0), (5, hb, PAD)):
                here = pl.ds(base + part_of * size, size)
                near[i, :, cols] = select(pick, layers, lambda x: buf[2, x, here, :], 3)

    def foresee():
        final = STEPS - 1

        def at(i, group):
            return near[i, pl.ds(group * rows, rows), :]

        def above(value):
            return jnp.where(line >= top, 0.0, pltpu.roll(value, rows - 1, 0))

        ex, ex_last, ex_next = at(0, 0), at(0, 1), at(0, 2)
        ey, ey_last, ey_next = at(1, 0), at(1, 1), at(1, 2)
        ez, ez_last = at(4, 0), at(4, 1)
        hx = at(2, 0) - DT * ((ahead(ez) - ez) - (ey_next - ey))
        hx_last = at(2, 1) - DT * ((ahead(ez_last) - ez_last) - (ey - ey_last))
        hy = at(3, 0) - DT * ((ex_next - ex) - (above(ez) - ez))
        hy_last = at(3, 1) - DT * ((ex - ex_last) - (above(ez_last) - ez_last))
        hz = at(5, 0) - DT * ((above(ey) - ey) - (ahead(ex) - ex))
        hz_below = jnp.where(line == 0, -lower * ey, pltpu.roll(hz, 1, 0))
        curl = (
            (hz - behind(hz)) - (hy - hy_last),
            (hx - hx_last) - (hz - hz_below),
        )
        products = [0.0] * 4
        for c, field in enumerate((ex, ey)):
            current = fixed[0] * memory[0, c] + fixed[1] * field - fixed[2] * memory[1, c]
            final_field = field + fixed[3] * (curl[c] - current)
            products[c] = products[c] + final_field * modes[c]
        products[2] = products[2] + hx * modes[2]
        products[3] = products[3] + hy * modes[3]

        @pl.when(has_upper)
        def _():
            weights_up().wait_send()
            weights_down().wait_recv()

        @pl.when(has_lower)
        def _():
            weights_down().wait_send()
            weights_up().wait_recv()

        def known(ref):
            return jnp.where(line < 4, ref[...].reshape(rows, width), 0.0)

        rise = jnp.where(line == 0, pltpu.roll(hz, rows - top, 0), 0.0)
        products[1] = products[1] + known(from_up) * rise
        step_x = (ey - behind(ey)) + (ez - ez_last)
        fall = placed([(DT * ez, 0), (-DT * step_x, 0), (DT * ey, 0)]) * known(from_down)
        for at_line, c in enumerate((3, 0, 1)):
            products[c] = products[c] + jnp.where(line == at_line, fall, 0.0)
        part[...] += sum(note(final, c, products[c]) for c in range(4))

    reach = [d for d in (4 << i for i in range(count.bit_length())) if d < count]

    def greet(i):
        for present, side in ((me >= reach[i], me - reach[i]), (me < count - reach[i], me + reach[i])):

            @pl.when(present)
            def _(side=side):
                pl.semaphore_signal(
                    met_sem.at[i], inc=1, device_id={"gx": side}, device_id_type=MESH
                )

    def met(i):
        peers = sum(p.astype(jnp.int32) for p in (me >= reach[i], me < count - reach[i]))
        pl.semaphore_wait(met_sem.at[i], peers)

    def due(n, c):
        return (n < STEPS - 2) | (c < CHUNKS - HELD)

    def send_up(n, c, slot):
        @pl.when(has_upper)
        def _():
            send_h(c, slot).wait_send()

        if isinstance(n, int):
            return
        partial_h(c * chunk, chunk)

        @pl.when(has_upper & due(n, c))
        def _():
            send_h(c, slot).start()

    to_scalars = pltpu.make_async_copy(rot, rot_s, rot_sem)
    to_scalars.start()

    def fold(begin, end):
        for c in range(4):

            def body(m, carry, c=c):
                here = pl.ds(pl.multiple_of(8 * m, 8), layers)
                plane = [planes[n, c, here, :] for n in range(begin, end)]
                for r in range(2):
                    for f in range(nf):
                        value = rot_s[r, f, begin * 4 + c] * plane[0]
                        for n in range(begin + 1, end):
                            value = value + rot_s[r, f, n * 4 + c] * plane[n - begin]
                        if begin > 0:
                            value = mon[r, c, f, m] + value
                        mon[r, c, f, m] = value
                return carry

            lax.fori_loop(0, nm, body, 0)

    def step(n, carry):
        last = isinstance(n, int)
        slot = n % 2 if last else lax.rem(n, 2)
        other = 1 - slot
        for c in range(CHUNKS):
            sweep(update_h, range(layers), c)

            @pl.when(has_upper)
            def _(c=c):
                send_e(c, eb, slot).wait_recv()

            @pl.when(has_lower)
            def _(c=c):
                send_h(c, slot).wait_recv()
                send_e(c, eb, slot).wait_send()

            finish_h(slot, c * chunk, chunk)
            sweep(update_e, (0, top), c, slot)

            if not last:

                @pl.when(has_lower & due(n, c))
                def _(c=c):
                    send_e(c, eb, other).start()

            if c > 0:
                send_up(n, c - 1, other)
            sweep(update_e, range(1, top), c, slot)
            if last and c == FOLD:
                to_scalars.wait()
                fold(0, STEPS - 1)
            if c == CHUNKS // 2 - 1:
                record_all(n, 0)
        send_up(n, CHUNKS - 1, other)
        record_all(n, 1)
        if last:
            return carry
        for i in range(min(len(reach), STEPS - 3)):

            @pl.when(n == i + 2)
            def _(i=i):
                if i > 0:
                    met(i - 1)
                greet(i)

        return carry

    lax.fori_loop(0, STEPS - 1, step, 0)
    foresee()

    begun = min(len(reach), STEPS - 3)
    for i in range(max(begun - 1, 0), len(reach)):
        if i >= begun:
            greet(i)
        met(i)

    def share(k, slot):
        return pltpu.make_async_remote_copy(
            src_ref=part,
            dst_ref=gathered.at[slot],
            send_sem=sp_sem,
            recv_sem=rp_sem,
            device_id={"gx": lax.rem(me + k, count)},
            device_id_type=MESH,
        )

    for k in range(1, count):
        share(k, me).start()
    for c in range(CHUNKS - HELD, CHUNKS):

        @pl.when(has_upper)
        def _(c=c):
            send_h(c, (STEPS - 1) % 2).start()

        @pl.when(has_lower)
        def _(c=c):
            send_e(c, eb, (STEPS - 1) % 2).start()

    gathered[me] = part[...]

    step(STEPS - 1, 0)
    fold(STEPS - 1, STEPS)

    others = gathered.at[pl.ds(0, count - 1)]
    arrivals = pltpu.make_async_remote_copy(
        src_ref=others,
        dst_ref=others,
        send_sem=sp_sem,
        recv_sem=rp_sem,
        device_id={"gx": lax.rem(me + 1, count)},
        device_id_type=MESH,
    )
    arrivals.wait_send()
    arrivals.wait_recv()
    total = gathered[0]
    for k in range(1, count):
        total = total + gathered[k]
    full[...] = total


def place_kernel(
    scale, eb, hb, mon, rot, full, el_out, ma_out, mon_out, inter_out, inter, sems
):
    width = el_out.shape[2]
    copies = [
        pltpu.make_async_copy(eb.at[:, :, pl.ds(0, width)], el_out, sems.at[0]),
        pltpu.make_async_copy(hb.at[:, :, pl.ds(PAD, width)], ma_out, sems.at[1]),
        pltpu.make_async_copy(mon, mon_out, sems.at[2]),
        pltpu.make_async_copy(inter, inter_out, sems.at[3]),
    ]
    for copy in copies[:3]:
        copy.start()
    for r in range(2):
        out = lax.dot_general(
            full[...],
            rot[r],
            (((1,), (1,)), ((), ())),
            preferred_element_type=F32,
            precision=lax.Precision.HIGHEST,
        )
        inter[r] = scale * out
    copies[3].start()
    for copy in copies:
        copy.wait()


def on_device(
    electric,
    magnetic,
    material,
    permittivity,
    pole_frequency,
    pole_damping,
    pole_strength,
    frequencies,
    plane_depth,
    mode_fields,
):
    count = lax.axis_size("gx")
    layers, width, deep = material.shape
    nm, nf = plane_depth.shape[0], frequencies.shape[0]
    scale = 1.0 / math.sqrt(4.0 * layers * count * width)

    smem = pl.BlockSpec(memory_space=pltpu.SMEM)
    vmem = pl.BlockSpec(memory_space=pltpu.VMEM)
    hbm = pl.BlockSpec(memory_space=pl.ANY)
    field = (3, layers, width, deep)
    padded = (3, layers, width + PAD, deep)
    final = (field, field, (2, 4, nf, nm, layers, width), (2, nm, nf))
    planar = (8 * nm, width)
    shapes = (padded, padded, final[2], (2, nf, deep), (nm, deep))
    kept = 4 * sum(math.prod(shape) for shape in shapes[:3]) + 2**17
    dma = pltpu.SemaphoreType.DMA
    held = pl.pallas_call(
        functools.partial(main_kernel, count),
        out_shape=tuple(pltpu.VMEM(shape, F32) for shape in shapes),
        in_specs=[smem] * 6 + [vmem] + [hbm] * 3,
        out_specs=(vmem,) * 5,
        scratch_shapes=[
            pltpu.VMEM((2, 2, width, deep), F32),
            pltpu.VMEM((2, 2, width, deep), F32),
            pltpu.VMEM((2, width, deep), F32),
            pltpu.VMEM(field, F32),
            pltpu.VMEM(field, F32),
            pltpu.VMEM((4, layers, width, deep), F32),
            pltpu.VMEM((layers, width, deep), jnp.int32),
            pltpu.VMEM((3 * 8 * nm, layers * 2 * deep), BF16),
            pltpu.VMEM((STEPS, 4) + planar, F32),
            pltpu.VMEM((4,) + planar, F32),
            pltpu.VMEM((4,) + planar, F32),
            pltpu.VMEM((2, 2) + planar, F32),
            pltpu.VMEM((6, 3 * 8 * nm, width), F32),
            pltpu.VMEM((nm, 8, width), F32),
            pltpu.VMEM((nm, 8, width), F32),
            pltpu.VMEM((nm, 8, width), F32),
            pltpu.VMEM((nm, 8, width), F32),
            pltpu.VMEM((nm, deep), F32),
            pltpu.VMEM((count, nm, deep), F32),
            pltpu.SMEM((2, nf, deep), F32),
            dma,
            dma((5,)),
            dma((CHUNKS,)),
            dma((2, CHUNKS)),
            dma((CHUNKS,)),
            dma((2, CHUNKS)),
            dma,
            dma,
            dma((4,)),
            pltpu.SemaphoreType.REGULAR((count.bit_length(),)),
        ],
        compiler_params=pltpu.CompilerParams(
            collective_id=0, has_side_effects=True, vmem_limit_bytes=VMEM_BYTES - kept
        ),
    )(
        permittivity,
        pole_frequency,
        pole_damping,
        pole_strength,
        frequencies,
        plane_depth,
        mode_fields,
        *(pltpu.with_memory_space_constraint(a, pltpu.HBM) for a in (electric, magnetic, material)),
    )
    return pl.pallas_call(
        functools.partial(place_kernel, scale),
        out_shape=tuple(jax.ShapeDtypeStruct(shape, F32) for shape in final),
        in_specs=[vmem] * 5,
        out_specs=(hbm,) * 4,
        scratch_shapes=[
            pltpu.VMEM(final[3], F32),
            dma((4,)),
        ],
        compiler_params=pltpu.CompilerParams(vmem_limit_bytes=16 * 2**20),
    )(*held)


def solution(mesh):
    in_specs = (
        P(None, "gx", None, None),
        P(None, "gx", None, None),
        P(("member", "gx"), None, None),
        P(),
        P(),
        P(),
        P(),
        P(),
        P(),
        P(None, None, "gx", None),
    )
    out_specs = (
        P(None, ("member", "gx"), None, None),
        P(None, ("member", "gx"), None, None),
        P(None, None, None, None, ("member", "gx"), None),
        P("member", None, None),
    )
    return jax.shard_map(
        on_device, mesh=mesh, in_specs=in_specs, out_specs=out_specs, check_vma=False
    )
```
